32 devices in a mesh: slab: 4 (over z), row: 2 (over core), pole: 4 (over y, x).
Axes of the slice: x: 2, y: 2, z: 4, core: 2. Of those that a mesh axis runs over, the one named last changes fastest.
Arguments:
- local_green: bfloat16 [2, 4, 2, 4096, 1024], P(None, 'pole', None, ('slab', 'row')), may hold values from -6 to 6
- coupling: bfloat16 [2, 4, 2, 4096, 1024], P(None, 'pole', None, ('slab', 'row')), may hold values from -0.1875 to 0.1875
- block_mask: int32 [2, 4, 32, 8], P(None, 'pole', ('slab', 'row')), may hold values from 0 to 1, as said below
- state_in: bfloat16 [4, 2, 4096, 1024], P('pole', None, ('slab', 'row')), may hold values from -6 to 6
- pole_weight: float32 [2, 16], replicated, may hold values from -4 to 4
- pole_index: int32 [2, 4, 4], P(None, 'pole', 'slab'), may hold values from 0 to 15
Outputs:
- state_out: bfloat16 [4, 2, 4096, 1024], P('pole', None, ('slab', 'row'))
- density: float32 [2, 4096, 1024], P(None, ('slab', 'row'), 'pole')
The draws below stay inside these ranges and needn't reach their ends.
Inputs may be any that keep to these rules, and one draw needn't show every extreme that they name: `block_mask`: every block row of every slab's mask has exactly 4 ones.
All inputs are finite; a program needn't handle non-finite values.
Results may differ from the reference program's by a relative error of at most 0.0095.
Values may be sent and summed in bfloat16 or wider, within the bound.
No kernel may reach another device: no remote copies, remote signals or barrier semaphores. Data moves between devices by JAX's collectives and lax.ppermute only.
A program may use at most 64 MiB of HBM per device.

```python
import jax
import jax.numpy as jnp
from jax import lax

BLK = 128
NBLK = 8
KEEP = 4
TICKS = 2
NTAB = 16
ORB = 1024
SLABS = 4
GROUPS = 4


def draw_block_mask(key, part):
    scores = jax.random.randint(key, (TICKS, GROUPS, SLABS * NBLK, NBLK), 0, 1 << 20) * NBLK
    scores = scores + jnp.arange(NBLK, dtype=jnp.int32)
    order = jnp.argsort(scores, axis=-1, stable=True)
    ranks = jnp.argsort(order, axis=-1, stable=True)
    return (ranks < KEEP).astype(jnp.int32)


def plant(values, own_key, smallest, top_value):
    extent = values.shape
    spot = [jax.random.randint(jax.random.fold_in(own_key, axis), (), 0, extent[axis]) for axis in range(len(extent))]
    values = values.at[tuple(spot)].set(smallest)
    longest = extent.index(max(extent))
    spot[longest] = (spot[longest] + 1) % extent[longest]
    return values.at[tuple(spot)].set(top_value)


def levels(rng, extent, cuts, smallest, top_value):
    def one(dim, parts):
        steps = jax.random.uniform(jax.random.fold_in(jax.random.fold_in(rng, 6), dim), (parts,), jnp.float32, smallest / len(cuts), top_value / len(cuts))
        return jnp.repeat(jnp.exp(steps), extent[dim] // parts).reshape((-1,) + (1,) * (len(extent) - dim - 1))

    level = one(*cuts[0])
    for cut in cuts[1:]:
        level = level * one(*cut)
    return level


def noise(stream_key, extent, deviation, bound, shards=(), kind=jnp.bfloat16):
    result = jax.random.normal(stream_key, extent, jnp.float32) * deviation
    if len(shards) > 0:
        result = levels(stream_key, extent, shards, -0.22, 0.18) * result
    return jnp.clip(result, min=-bound, max=bound).astype(kind)


def setup_inputs(seed: int = 0) -> dict:
    splits = jax.random.split(jax.random.key(seed), 7)
    local_green = noise(splits[0], (TICKS, GROUPS, 2, SLABS * ORB, ORB), 1.0, 6.0, ((1, 4), (3, 8)))
    coupling = noise(splits[1], (TICKS, GROUPS, 2, SLABS * ORB, ORB), ORB ** -0.5, 0.1875, ((1, 4), (3, 8)))
    block_mask = draw_block_mask(jax.random.fold_in(splits[6], 71), 0)
    state_in = noise(splits[3], (GROUPS, 2, SLABS * ORB, ORB), 1.0, 6.0, ((0, 4), (2, 8)))
    pole_weight = noise(splits[4], (2, NTAB), 1.0, 4.0, (), jnp.float32)
    pole_index = plant(jax.random.randint(splits[5], (TICKS, GROUPS, SLABS), 0, NTAB), jax.random.fold_in(splits[5], 1), 0, NTAB - 1).astype(jnp.int32)
    return dict(local_green=local_green, coupling=coupling, block_mask=block_mask, state_in=state_in, pole_weight=pole_weight, pole_index=pole_index)


def expand_mask(mask_rows):
    count = mask_rows.shape[0]
    wide = jnp.broadcast_to(mask_rows[:, None, :, None], (count, BLK, NBLK, BLK))
    return wide.reshape(count * BLK, NBLK * BLK)


def complex_left(first, second):
    f0 = first[0].astype(jnp.float32)
    f1 = first[1].astype(jnp.float32)
    s0 = second[0].astype(jnp.float32)
    s1 = second[1].astype(jnp.float32)
    real_part = jnp.einsum('sij,sjk->sik', f0, s0) - jnp.einsum('sij,sjk->sik', f1, s1)
    imag_part = jnp.einsum('sij,sjk->sik', f0, s1) + jnp.einsum('sij,sjk->sik', f1, s0)
    return jnp.stack([real_part, imag_part])


def complex_right(first, second):
    f0 = first[0].astype(jnp.float32)
    f1 = first[1].astype(jnp.float32)
    s0 = second[0].astype(jnp.float32)
    s1 = second[1].astype(jnp.float32)
    real_part = jnp.einsum('sik,sjk->sij', f0, s0) - jnp.einsum('sik,sjk->sij', f1, s1)
    imag_part = jnp.einsum('sik,sjk->sij', f0, s1) + jnp.einsum('sik,sjk->sij', f1, s0)
    return jnp.stack([real_part, imag_part])


def reference(local_green, coupling, block_mask, state_in, pole_weight, pole_index):
    orbitals = NBLK * BLK
    density = jnp.zeros((2, SLABS * orbitals, orbitals), jnp.float32)
    finals = []
    for group in range(GROUPS):
        state = state_in[group]
        for tick in range(TICKS):
            dense_mask = expand_mask(block_mask[tick, group]).astype(jnp.bfloat16)
            masked = coupling[tick, group] * dense_mask[None]
            upper = masked.reshape(2, SLABS, orbitals, orbitals)
            previous = state.reshape(2, SLABS, orbitals, orbitals)
            incoming = jnp.concatenate([previous[:, 1:], jnp.zeros((2, 1, orbitals, orbitals), jnp.bfloat16)], axis=1)
            half = complex_left(upper, incoming).astype(jnp.bfloat16)
            half = lax.optimization_barrier(half)
            sandwich = complex_right(half, upper).reshape(2, SLABS * orbitals, orbitals)
            green = (local_green[tick, group].astype(jnp.float32) + sandwich).astype(jnp.bfloat16)
            weights = pole_weight[:, pole_index[tick, group]]
            weights = jnp.repeat(weights, orbitals, axis=1)[:, :, None]
            green_real = green[0].astype(jnp.float32)
            green_imag = green[1].astype(jnp.float32)
            term = jnp.stack([weights[0] * green_real - weights[1] * green_imag,
                              weights[0] * green_imag + weights[1] * green_real]).astype(jnp.bfloat16)
            term = lax.optimization_barrier(term)
            density = density + term.astype(jnp.float32)
            state = green
        finals.append(state)
    return jnp.stack(finals), density
```

```python
import functools

import jax
import jax.numpy as jnp
from jax import lax
from jax.experimental import pallas as pl
from jax.experimental.pallas import tpu as pltpu
from jax.sharding import PartitionSpec as P


BF16 = jnp.bfloat16
F32 = jnp.float32

LIMIT = pltpu.CompilerParams(vmem_limit_bytes=20 << 20)


def from_behind(block, axis):
    devices = range(lax.axis_size(axis))
    return lax.ppermute(block, axis, [(i + 1, i) for i in devices if i + 1 in devices])


def flip(block, axis, bit):
    return lax.ppermute(block, axis, [(i, i ^ bit) for i in range(lax.axis_size(axis))])


def row_pieces(block):
    rows = block.shape[1]
    count = lax.axis_size("row")
    if count == 1:
        return [block], [0]
    if count == 2:
        here = lax.axis_index("row")
        there = flip(block, "row", 1)
        return [block, there], [here * rows, (1 - here) * rows]
    return [lax.all_gather(block, "row", axis=1, tiled=True)], [0]


def mask_body(mask_ref, coupling_ref, out_ref, *, tick, per_tile):
    tile = pl.program_id(0)
    blocks = mask_ref.shape[3]
    wide = coupling_ref.shape[4] // blocks
    high = coupling_ref.shape[3] // per_tile
    for part in range(per_tile):
        rows = slice(part * high, (part + 1) * high)
        for col in range(blocks):
            cols = slice(col * wide, (col + 1) * wide)
            keep = mask_ref[tick, 0, tile * per_tile + part, col] != 0
            block = coupling_ref[0, 0, :, rows, cols]
            out_ref[:, rows, cols] = jnp.where(keep, block, jnp.zeros_like(block))


def masked_factor(block_mask, coupling, tick):
    rows, width = coupling.shape[3:]
    block_rows = block_mask.shape[2]
    per_tile = 2 if block_rows % 2 == 0 else 1
    tile = rows // block_rows * per_tile
    return pl.pallas_call(
        functools.partial(mask_body, tick=tick, per_tile=per_tile),
        grid_spec=pltpu.PrefetchScalarGridSpec(
            num_scalar_prefetch=1,
            grid=(rows // tile,),
            in_specs=[pl.BlockSpec((1, 1, 2, tile, width), lambda i, m: (tick, 0, 0, i, 0))],
            out_specs=pl.BlockSpec((2, tile, width), lambda i, m: (0, i, 0)),
        ),
        out_shape=jax.ShapeDtypeStruct((2, rows, width), BF16),
        compiler_params=LIMIT,
    )(block_mask, coupling)


def dot(a, b):
    return jnp.dot(a, b, preferred_element_type=F32)


def dot_t(a, b):
    return lax.dot_general(a, b, (((1,), (1,)), ((), ())), preferred_element_type=F32)


def fold_body(*refs, pieces, tick, first, last, start_of_term):
    offs, pidx, pw, here = refs[:4]
    refs = refs[4:]
    own = refs[0]
    factor = refs[1 : 1 + pieces]
    behind = refs[1 + pieces : 1 + 2 * pieces]
    before = refs[1 + 2 * pieces]
    outs = refs[2 + 2 * pieces : -3]
    right, low, high = refs[-3:]
    span = behind[0].shape[2]

    @pl.when(pl.program_id(0) == 0)
    def _():
        for k in range(pieces):
            size = behind[k].shape[1]
            at = pl.ds(pl.multiple_of(offs[k], size), size)
            right[at, :span] = behind[k][0]
            right[at, span:] = behind[k][1]
            low[at, :span] = factor[k][0]
            low[at, span:] = -factor[k][1]
            high[at, :span] = factor[k][1]
            high[at, span:] = factor[k][0]

    a = dot(own[0], right[...])
    b = dot(own[1], right[...])
    half = jnp.concatenate([a[:, :span] - b[:, span:], a[:, span:] + b[:, :span]], axis=1).astype(BF16)
    if first:
        old = (before[0, 0, 0].astype(F32), before[0, 0, 1].astype(F32))
    else:
        old = (before[0], before[1])
    real = old[0] + dot_t(half, low[...])
    imag = old[1] + dot_t(half, high[...])
    if not last:
        outs[0][0] = real
        outs[0][1] = imag
        return
    real = real.astype(BF16)
    imag = imag.astype(BF16)
    start = 0
    for out in outs[:start_of_term]:
        cols = slice(start, start + out.shape[2])
        out[0] = real[:, cols]
        out[1] = imag[:, cols]
        start += out.shape[2]
    if len(outs) > start_of_term:
        write_term(real, imag, pidx, pw, here, tick, outs[start_of_term:])


def write_term(real, imag, pidx, pw, here, tick, outs):
    real = real.astype(F32)
    imag = imag.astype(F32)
    w0 = pw[0, pidx[tick, 0, 0]]
    w1 = pw[1, pidx[tick, 0, 0]]
    term_real = (w0 * real - w1 * imag).astype(BF16)
    term_imag = (w0 * imag + w1 * real).astype(BF16)
    if len(outs) == 1:
        outs[0][0] = term_real
        outs[0][1] = term_imag
        return
    real_send, real_keep, imag_send, imag_keep = outs
    quarter = term_real.shape[1] // 4
    first_major = here[0] // 2 == 0
    first_minor = here[0] % 2 == 0
    lower, upper = term_real[:, : 2 * quarter], term_real[:, 2 * quarter :]
    real_send[...] = jnp.where(first_major, upper, lower)
    real_keep[...] = jnp.where(first_major, lower, upper)
    for pair in range(2):
        at = slice(pair * quarter, (pair + 1) * quarter)
        even = term_imag[:, 2 * pair * quarter : (2 * pair + 1) * quarter]
        odd = term_imag[:, (2 * pair + 1) * quarter : (2 * pair + 2) * quarter]
        imag_send[:, at] = jnp.where(first_minor, odd, even)
        imag_keep[:, at] = jnp.where(first_minor, even, odd)


def term_outs(rows, width, tile):
    if lax.axis_size("pole") == 4:
        spec = pl.BlockSpec((tile, width // 2), lambda i, *_: (i, 0))
        return [spec] * 4, [jax.ShapeDtypeStruct((rows, width // 2), BF16)] * 4
    spec = pl.BlockSpec((2, tile, width), lambda i, *_: (0, i, 0))
    return [spec], [jax.ShapeDtypeStruct((2, rows, width), BF16)]


def fold(scalars, own, factor, behind, before, tick, chunk, first, last, widths, with_term):
    rows, width = own.shape[1:]
    span = behind[0].shape[2]
    tile = min(rows, 256)
    pieces = len(behind)
    flat = pl.BlockSpec((2, tile, width), lambda i, *_: (0, i, 0))
    once = pl.Buffered(1)
    in_specs = [flat]
    for piece in factor:
        in_specs.append(pl.BlockSpec((2, piece.shape[1], span), lambda i, *_: (0, 0, chunk), pipeline_mode=once))
    for piece in behind:
        in_specs.append(pl.BlockSpec(memory_space=pltpu.VMEM))
    if first:
        in_specs.append(pl.BlockSpec((1, 1, 2, tile, width), lambda i, *_: (tick, 0, 0, i, 0)))
    else:
        in_specs.append(flat)
    if last:
        out_specs = [pl.BlockSpec((2, tile, w), lambda i, *_: (0, i, 0)) for w in widths]
        out_shape = [jax.ShapeDtypeStruct((2, rows, w), BF16) for w in widths]
        if with_term:
            more = term_outs(rows, width, tile)
            out_specs += more[0]
            out_shape += more[1]
    else:
        out_specs = [flat]
        out_shape = [jax.ShapeDtypeStruct((2, rows, width), F32)]
    aliases = {} if first or last else {len(scalars) + 1 + 2 * pieces: 0}
    return pl.pallas_call(
        functools.partial(
            fold_body, pieces=pieces, tick=tick, first=first, last=last, start_of_term=len(widths)
        ),
        grid_spec=pltpu.PrefetchScalarGridSpec(
            num_scalar_prefetch=len(scalars),
            grid=(rows // tile,),
            in_specs=in_specs,
            out_specs=out_specs,
            scratch_shapes=[pltpu.VMEM((width, 2 * span), BF16)] * 3,
        ),
        out_shape=out_shape,
        input_output_aliases=aliases,
        compiler_params=LIMIT,
    )(*scalars, own, *factor, *behind, before)


def term_body(pidx, pw, here, *refs, tick, count):
    real = jnp.concatenate([ref[0] for ref in refs[:count]], axis=1)
    imag = jnp.concatenate([ref[1] for ref in refs[:count]], axis=1)
    write_term(real, imag, pidx, pw, here, tick, refs[count:])


def weigh(scalars, state, tick):
    rows = state[0].shape[1]
    tile = min(rows, 256)
    out_specs, out_shape = term_outs(rows, sum(piece.shape[2] for piece in state), tile)
    return pl.pallas_call(
        functools.partial(term_body, tick=tick, count=len(state)),
        grid_spec=pltpu.PrefetchScalarGridSpec(
            num_scalar_prefetch=3,
            grid=(rows // tile,),
            in_specs=[pl.BlockSpec((2, tile, p.shape[2]), lambda i, *_: (0, i, 0)) for p in state],
            out_specs=out_specs,
        ),
        out_shape=out_shape,
        compiler_params=LIMIT,
    )(*scalars[1:], *state)


def cut_body(src, out):
    out[...] = src[0]


def first_piece(state, span):
    rows = state.shape[2]
    return pl.pallas_call(
        cut_body,
        grid=(1,),
        in_specs=[pl.BlockSpec((1, 2, rows, span), lambda i: (0, 0, 0, 0))],
        out_specs=pl.BlockSpec((2, rows, span), lambda i: (0, 0, 0)),
        out_shape=jax.ShapeDtypeStruct((2, rows, span), BF16),
        compiler_params=LIMIT,
        name="cut",
    )(state)


def pass_on_body(here, real_keep, real_got, imag_keep, imag_got, real_send, imag_send):
    real_send[...] = (real_keep[...].astype(F32) + real_got[...].astype(F32)).astype(BF16)
    imag_send[...] = (imag_keep[...].astype(F32) + imag_got[...].astype(F32)).astype(BF16)


def retain_body(here, real_keep, real_got, imag_keep, imag_got, *refs):
    out = refs[-1]
    real = real_keep[...].astype(F32) + real_got[...].astype(F32)
    imag = imag_keep[...].astype(F32) + imag_got[...].astype(F32)
    if len(refs) == 2:
        real = refs[0][0] + real
        imag = refs[0][1] + imag
    out[0] = real
    out[1] = imag


def close_body(base, real_last, imag_last, out):
    out[0] = base[0] + real_last[...].astype(F32)
    out[1] = base[1] + imag_last[...].astype(F32)


def scatter_sum(parts, before, here):
    if len(parts) == 1:
        share = lax.psum_scatter(parts[0], "pole", scatter_dimension=2, tiled=True).astype(F32)
        return share if before is None else before + share
    real_out, real_keep, imag_out, imag_keep = parts
    rows, half = real_out.shape
    quarter = half // 2
    tile = min(rows, 256)
    real_got = flip(real_out, "pole", 2)
    imag_got = flip(imag_out, "pole", 1)
    fields = (real_keep, real_got, imag_keep, imag_got)
    block = (tile, quarter)

    def picked(mine):
        real_at = pl.BlockSpec(block, lambda i, h: (i, h[0] % 2 if mine else 1 - h[0] % 2))
        imag_at = pl.BlockSpec(block, lambda i, h: (i, h[0] // 2 if mine else 1 - h[0] // 2))
        return [real_at, real_at, imag_at, imag_at]

    flat = pl.BlockSpec(block, lambda i, *_: (i, 0))
    both = pl.BlockSpec((2, tile, quarter), lambda i, *_: (0, i, 0))
    real_send, imag_send = pl.pallas_call(
        pass_on_body,
        grid_spec=pltpu.PrefetchScalarGridSpec(
            num_scalar_prefetch=1, grid=(rows // tile,), in_specs=picked(False), out_specs=[flat, flat]
        ),
        out_shape=[jax.ShapeDtypeStruct((rows, quarter), BF16)] * 2,
        compiler_params=LIMIT,
    )(here, *fields)
    real_last = flip(real_send, "pole", 1)
    imag_last = flip(imag_send, "pole", 2)
    extra = [] if before is None else [before]
    shape = jax.ShapeDtypeStruct((2, rows, quarter), F32)
    base = pl.pallas_call(
        retain_body,
        grid_spec=pltpu.PrefetchScalarGridSpec(
            num_scalar_prefetch=1, grid=(rows // tile,), in_specs=picked(True) + [both] * len(extra), out_specs=both
        ),
        out_shape=shape,
        compiler_params=LIMIT,
    )(here, *fields, *extra)
    return pl.pallas_call(
        close_body,
        grid=(rows // tile,),
        in_specs=[both, flat, flat],
        out_specs=both,
        out_shape=shape,
        compiler_params=LIMIT,
    )(base, real_last, imag_last)


def body(local_green, coupling, block_mask, state_in, pole_weight, pole_index):
    ticks = coupling.shape[0]
    width = coupling.shape[4]
    span = min(128, width)
    chunks = width // span
    state = [first_piece(state_in, span)]
    state += [state_in[0, :, :, c * span : (c + 1) * span] for c in range(1, chunks)]
    here = jnp.reshape(lax.axis_index("pole").astype(jnp.int32), (1,))
    factors = []
    density = None
    for tick in range(ticks):
        own = masked_factor(block_mask, coupling, tick)
        factors.append((own, *row_pieces(own)))
    for tick in range(ticks):
        incoming = []
        for c in range(chunks):
            incoming.append(from_behind(state[c], "slab"))
        own, factor, offsets = factors[tick]
        scalars = (jnp.stack([jnp.int32(o) for o in offsets]), pole_index, pole_weight, here)
        before = local_green
        last_tick = tick == ticks - 1
        widths = [width] if last_tick else [span] * chunks
        for c in range(chunks):
            behind, _ = row_pieces(incoming[c])
            last = c == chunks - 1
            outs = fold(
                scalars, own, factor, behind, before, tick, c, c == 0, last, widths if last else [], last_tick
            )
            before = outs[0]
        state = outs[: len(widths)]
        parts = outs[len(widths) :] or weigh(scalars, state, tick)
        density = scatter_sum(parts, density, here)
    return (state[0][None], density)


def solution(mesh):
    placed = (
        P(None, "pole", None, ("slab", "row"), None),
        P(None, "pole", None, ("slab", "row"), None),
        P(None, "pole", ("slab", "row"), None),
        P("pole", None, ("slab", "row"), None),
        P(),
        P(None, "pole", "slab"),
    )
    return jax.shard_map(
        body,
        mesh=mesh,
        in_specs=placed,
        out_specs=(P("pole", None, ("slab", "row"), None), P(None, ("slab", "row"), "pole")),
        check_vma=False,
    )
```

```python
import functools

import jax
import jax.numpy as jnp
from jax import lax
from jax.experimental import pallas as pl
from jax.experimental.pallas import tpu as pltpu
from jax.sharding import PartitionSpec as P


BF16 = jnp.bfloat16
F32 = jnp.float32

LIMIT = pltpu.CompilerParams(vmem_limit_bytes=20 << 20)


def from_behind(block, axis):
    devices = range(lax.axis_size(axis))
    return lax.ppermute(block, axis, [(i + 1, i) for i in devices if i + 1 in devices])


def flip(block, axis, bit):
    return lax.ppermute(block, axis, [(i, i ^ bit) for i in range(lax.axis_size(axis))])


def row_pieces(block):
    rows = block.shape[1]
    count = lax.axis_size("row")
    if count == 1:
        return [block], [0]
    if count == 2:
        here = lax.axis_index("row")
        there = flip(block, "row", 1)
        return [block, there], [here * rows, (1 - here) * rows]
    return [lax.all_gather(block, "row", axis=1, tiled=True)], [0]


VMEM = pl.BlockSpec(memory_space=pltpu.VMEM)
HBM = pl.BlockSpec(memory_space=pltpu.HBM)


def mask_body(mask_ref, coupling_ref, out_ref, sems, *, tick):
    block_rows, blocks = mask_ref.shape[2:]
    rows, width = out_ref.shape[1:]
    high, wide = rows // block_rows, width // blocks

    def fetch(k):
        at = pl.ds(k * high, high)
        return pltpu.make_async_copy(coupling_ref.at[tick, 0, :, at, :], out_ref.at[:, at, :], sems.at[k])

    for k in range(block_rows):
        fetch(k).start()
    for k in range(block_rows):
        fetch(k).wait()
        rows_at = slice(k * high, (k + 1) * high)
        for col in range(blocks):
            cols = slice(col * wide, (col + 1) * wide)
            block = out_ref[:, rows_at, cols]
            keep = mask_ref[tick, 0, k, col] != 0
            out_ref[:, rows_at, cols] = jnp.where(keep, block, jnp.zeros_like(block))


def masked_factor(block_mask, coupling, tick):
    rows, width = coupling.shape[3:]
    return pl.pallas_call(
        functools.partial(mask_body, tick=tick),
        grid_spec=pltpu.PrefetchScalarGridSpec(
            num_scalar_prefetch=1,
            grid=(1,),
            in_specs=[HBM],
            out_specs=VMEM,
            scratch_shapes=[pltpu.SemaphoreType.DMA((block_mask.shape[2],))],
        ),
        out_shape=jax.ShapeDtypeStruct((2, rows, width), BF16),
        compiler_params=LIMIT,
    )(block_mask, coupling)


def dot(a, b):
    return jnp.dot(a, b, preferred_element_type=F32)


def dot_t(a, b):
    return lax.dot_general(a, b, (((1,), (1,)), ((), ())), preferred_element_type=F32)


def fold_body(*refs, pieces, tick, start, first, last, chunks):
    offs, pidx, pw, here = refs[:4]
    refs = refs[4:]
    own = refs[0]
    factor = refs[1 : 1 + pieces]
    behind = refs[1 + pieces : 1 + 2 * pieces]
    before = refs[1 + 2 * pieces]
    right, low, high = refs[-3:]
    outs = refs[2 + 2 * pieces : -3]
    rows = own.shape[1]
    span = behind[0].shape[2]
    if first:
        green, sem = outs[-2:]
        outs = outs[:-2]
        fetch = pltpu.make_async_copy(before.at[tick, 0], green, sem)
        fetch.start()
    cols = slice(start, start + span)
    for k in range(pieces):
        size = behind[k].shape[1]
        at = pl.ds(pl.multiple_of(offs[k], size), size)
        right[at, :span] = behind[k][0]
        right[at, span:] = behind[k][1]
        low[at, :span] = factor[k][0, :, cols]
        low[at, span:] = -factor[k][1, :, cols]
        high[at, :span] = factor[k][1, :, cols]
        high[at, span:] = factor[k][0, :, cols]
    tile = min(rows, 256)
    for step in range(rows // tile):
        at = slice(step * tile, (step + 1) * tile)
        a = dot(own[0, at], right[...])
        b = dot(own[1, at], right[...])
        half = jnp.concatenate([a[:, :span] - b[:, span:], a[:, span:] + b[:, :span]], axis=1).astype(BF16)
        real = dot_t(half, low[...])
        imag = dot_t(half, high[...])
        if first:
            if step == 0:
                fetch.wait()
            real = green[0, at].astype(F32) + real
            imag = green[1, at].astype(F32) + imag
        else:
            real = before[0, at] + real
            imag = before[1, at] + imag
        if not last:
            outs[0][0, at] = real
            outs[0][1, at] = imag
            continue
        real = real.astype(BF16)
        imag = imag.astype(BF16)
        left = 0
        for out in outs[:chunks]:
            out[0, at] = real[:, left : left + out.shape[2]]
            out[1, at] = imag[:, left : left + out.shape[2]]
            left += out.shape[2]
        if len(outs) > chunks:
            write_term(real, imag, pidx, pw, here, tick, outs[chunks:], step * tile)


def write_term(real, imag, pidx, pw, here, tick, outs, row):
    real = real.astype(F32)
    imag = imag.astype(F32)
    w0 = pw[0, pidx[tick, 0, 0]]
    w1 = pw[1, pidx[tick, 0, 0]]
    term_real = (w0 * real - w1 * imag).astype(BF16)
    term_imag = (w0 * imag + w1 * real).astype(BF16)
    high, width = real.shape
    if len(outs) == 1:
        outs[0][0, row : row + high] = term_real
        outs[0][1, row : row + high] = term_imag
        return
    part = row // outs[0].shape[0]
    row -= part * outs[0].shape[0]
    at = slice(row, row + high)
    real_send, real_keep, imag_send, imag_keep = outs[4 * part : 4 * part + 4]
    quarter = width // 4
    first_major = here[0] // 2 == 0
    first_minor = here[0] % 2 == 0
    lower, upper = term_real[:, : 2 * quarter], term_real[:, 2 * quarter :]
    real_send[at] = jnp.where(first_major, upper, lower)
    real_keep[at] = jnp.where(first_major, lower, upper)
    for pair in range(2):
        cols = slice(pair * quarter, (pair + 1) * quarter)
        even = term_imag[:, 2 * pair * quarter : (2 * pair + 1) * quarter]
        odd = term_imag[:, (2 * pair + 1) * quarter : (2 * pair + 2) * quarter]
        imag_send[at, cols] = jnp.where(first_minor, odd, even)
        imag_keep[at, cols] = jnp.where(first_minor, even, odd)


def term_shapes(rows, width):
    if lax.axis_size("pole") != 4:
        return [jax.ShapeDtypeStruct((2, rows, width), BF16)]
    parts = 2 if rows % 512 == 0 else 1
    return [jax.ShapeDtypeStruct((rows // parts, width // 2), BF16)] * (4 * parts)


def fold(scalars, own, factor, behind, before, tick, start, first, last, widths, with_term):
    rows, width = own.shape[1:]
    span = behind[0].shape[2]
    pieces = len(behind)
    if last:
        out_shape = [jax.ShapeDtypeStruct((2, rows, w), BF16) for w in widths]
        if with_term:
            out_shape += term_shapes(rows, width)
    else:
        out_shape = [jax.ShapeDtypeStruct((2, rows, width), F32)]
    scratch = [pltpu.VMEM((2, rows, width), BF16), pltpu.SemaphoreType.DMA] if first else []
    return pl.pallas_call(
        functools.partial(
            fold_body, pieces=pieces, tick=tick, start=start, first=first, last=last, chunks=len(widths)
        ),
        grid_spec=pltpu.PrefetchScalarGridSpec(
            num_scalar_prefetch=len(scalars),
            grid=(1,),
            in_specs=[VMEM] * (1 + 2 * pieces) + [HBM if first else VMEM],
            out_specs=[VMEM] * len(out_shape),
            scratch_shapes=scratch + [pltpu.VMEM((width, 2 * span), BF16)] * 3,
        ),
        out_shape=out_shape,
        input_output_aliases={} if first or last else {len(scalars) + 1 + 2 * pieces: 0},
        compiler_params=LIMIT,
    )(*scalars, own, *factor, *behind, before)


def term_body(pidx, pw, here, *refs, tick, count):
    rows = refs[0].shape[1]
    tile = min(rows, 256)
    for row in range(0, rows, tile):
        real = jnp.concatenate([ref[0, row : row + tile] for ref in refs[:count]], axis=1)
        imag = jnp.concatenate([ref[1, row : row + tile] for ref in refs[:count]], axis=1)
        write_term(real, imag, pidx, pw, here, tick, refs[count:], row)


def weigh(scalars, state, tick):
    out_shape = term_shapes(state[0].shape[1], sum(piece.shape[2] for piece in state))
    return pl.pallas_call(
        functools.partial(term_body, tick=tick, count=len(state)),
        grid_spec=pltpu.PrefetchScalarGridSpec(
            num_scalar_prefetch=3,
            grid=(1,),
            in_specs=[VMEM] * len(state),
            out_specs=[VMEM] * len(out_shape),
        ),
        out_shape=out_shape,
        compiler_params=LIMIT,
    )(*scalars[1:], *state)


def cut_body(src, out, sem, *, start):
    fetch = pltpu.make_async_copy(src.at[0, :, :, pl.ds(start, out.shape[2])], out, sem)
    fetch.start()
    fetch.wait()


def cut_piece(state, start, span):
    return pl.pallas_call(
        functools.partial(cut_body, start=start),
        in_specs=[HBM],
        out_specs=VMEM,
        out_shape=jax.ShapeDtypeStruct((2, state.shape[2], span), BF16),
        scratch_shapes=[pltpu.SemaphoreType.DMA],
        compiler_params=LIMIT,
    )(state)


def picked(ref, which):
    quarter = ref.shape[1] // 2
    return jnp.where(which == 0, ref[:, :quarter], ref[:, quarter:]).astype(F32)


def pass_on_body(here, real_keep, real_got, imag_keep, imag_got, real_send, imag_send):
    major, minor = here[0] // 2, here[0] % 2
    real_send[...] = (picked(real_keep, 1 - minor) + picked(real_got, 1 - minor)).astype(BF16)
    imag_send[...] = (picked(imag_keep, 1 - major) + picked(imag_got, 1 - major)).astype(BF16)


def retain_body(here, *refs, parts, extra):
    major, minor = here[0] // 2, here[0] % 2
    out = refs[-1]
    high = refs[0].shape[0]
    for k in range(parts):
        real_keep, real_got, imag_keep, imag_got = refs[4 * k : 4 * k + 4]
        at = slice(k * high, (k + 1) * high)
        real = picked(real_keep, minor) + picked(real_got, minor)
        imag = picked(imag_keep, major) + picked(imag_got, major)
        if extra:
            real = refs[4 * parts][0, at] + real
            imag = refs[4 * parts][1, at] + imag
        out[0, at] = real
        out[1, at] = imag


def close_body(base, *refs):
    out = refs[-1]
    parts = len(refs) // 2
    high = refs[0].shape[0]
    for k in range(parts):
        at = slice(k * high, (k + 1) * high)
        out[0, at] = base[0, at] + refs[2 * k][...].astype(F32)
        out[1, at] = base[1, at] + refs[2 * k + 1][...].astype(F32)


def kernel_call(fn, scalars, args, out_shape):
    many = isinstance(out_shape, list)
    return pl.pallas_call(
        fn,
        grid_spec=pltpu.PrefetchScalarGridSpec(
            num_scalar_prefetch=len(scalars),
            grid=(1,),
            in_specs=[VMEM] * len(args),
            out_specs=[VMEM] * len(out_shape) if many else VMEM,
        ),
        out_shape=out_shape,
        compiler_params=LIMIT,
    )(*scalars, *args)


def scatter_sum(terms, before, here):
    if len(terms) == 1:
        share = lax.psum_scatter(terms[0], "pole", scatter_dimension=2, tiled=True).astype(F32)
        return share if before is None else before + share
    parts = len(terms) // 4
    high, half = terms[0].shape
    quarter = half // 2
    fields = []
    for k in range(parts):
        real_out, real_keep, imag_out, imag_keep = terms[4 * k : 4 * k + 4]
        real_got = flip(real_out, "pole", 2)
        imag_got = flip(imag_out, "pole", 1)
        fields.append((real_keep, real_got, imag_keep, imag_got))
    lasts = []
    for k in range(parts):
        sends = kernel_call(
            pass_on_body, (here,), fields[k], [jax.ShapeDtypeStruct((high, quarter), BF16)] * 2
        )
        lasts.append(flip(sends[0], "pole", 1))
        lasts.append(flip(sends[1], "pole", 2))
    extra = [] if before is None else [before]
    shape = jax.ShapeDtypeStruct((2, parts * high, quarter), F32)
    flat = [value for field in fields for value in field]
    retain = functools.partial(retain_body, parts=parts, extra=len(extra))
    base = kernel_call(retain, (here,), flat + extra, shape)
    return kernel_call(close_body, (), [base, *lasts], shape)


def spans(width):
    unit = width // 8
    if unit % 128:
        return [width]
    return [3 * unit, 2 * unit, 2 * unit, unit]


def body(local_green, coupling, block_mask, state_in, pole_weight, pole_index):
    local_green, coupling, state_in = (
        pltpu.with_memory_space_constraint(value, pltpu.HBM) for value in (local_green, coupling, state_in)
    )
    ticks = coupling.shape[0]
    width = coupling.shape[4]
    sizes = spans(width)
    starts = [sum(sizes[:c]) for c in range(len(sizes))]
    state = []
    for c, start in enumerate(starts):
        state.append(cut_piece(state_in, start, sizes[c]))
    here = jnp.reshape(lax.axis_index("pole").astype(jnp.int32), (1,))
    factors = []
    density = None
    for tick in range(ticks):
        own = masked_factor(block_mask, coupling, tick)
        factors.append((own, *row_pieces(own)))
    for tick in range(ticks):
        incoming = []
        for c in range(len(sizes)):
            incoming.append(from_behind(state[c], "slab"))
        own, factor, offsets = factors[tick]
        scalars = (jnp.stack([jnp.int32(o) for o in offsets]), pole_index, pole_weight, here)
        before = local_green
        last_tick = tick == ticks - 1
        widths = [width] if last_tick else sizes
        for c, start in enumerate(starts):
            behind, _ = row_pieces(incoming[c])
            last = c == len(sizes) - 1
            outs = fold(
                scalars, own, factor, behind, before, tick, start, c == 0, last, widths if last else [], last_tick
            )
            before = outs[0]
        state = outs[: len(widths)]
        terms = outs[len(widths) :] or weigh(scalars, state, tick)
        density = scatter_sum(terms, density, here)
    return (state[0][None], density)


def solution(mesh):
    placed = (
        P(None, "pole", None, ("slab", "row"), None),
        P(None, "pole", None, ("slab", "row"), None),
        P(None, "pole", ("slab", "row"), None),
        P("pole", None, ("slab", "row"), None),
        P(),
        P(None, "pole", "slab"),
    )
    return jax.shard_map(
        body,
        mesh=mesh,
        in_specs=placed,
        out_specs=(P("pole", None, ("slab", "row"), None), P(None, ("slab", "row"), "pole")),
        check_vma=False,
    )
```

```python
import functools

import jax
import jax.numpy as jnp
from jax import lax
from jax.experimental import pallas as pl
from jax.experimental.pallas import tpu as pltpu
from jax.sharding import PartitionSpec as P


BF16 = jnp.bfloat16
F32 = jnp.float32

LIMIT = pltpu.CompilerParams(vmem_limit_bytes=20 << 20)


def from_behind(block, axis):
    devices = range(lax.axis_size(axis))
    return lax.ppermute(block, axis, [(i + 1, i) for i in devices if i + 1 in devices])


def flip(block, axis, bit):
    return lax.ppermute(block, axis, [(i, i ^ bit) for i in range(lax.axis_size(axis))])


def row_pieces(block):
    count = lax.axis_size("row")
    if count == 1:
        return [block]
    if count == 2:
        there = flip(block, "row", 1)
        return [block, there]
    return [lax.all_gather(block, "row", axis=1, tiled=True)]


VMEM = pl.BlockSpec(memory_space=pltpu.VMEM)
HBM = pl.BlockSpec(memory_space=pltpu.HBM)


def mask_body(mask_ref, coupling_ref, out_ref, sems, *, tick):
    block_rows, blocks = mask_ref.shape[2:]
    rows, width = out_ref.shape[1:]
    high, wide = rows // block_rows, width // blocks

    def fetch(k):
        at = pl.ds(k * high, high)
        return pltpu.make_async_copy(coupling_ref.at[tick, 0, :, at, :], out_ref.at[:, at, :], sems.at[k])

    for k in range(block_rows):
        fetch(k).start()
    for k in range(block_rows):
        fetch(k).wait()
        rows_at = slice(k * high, (k + 1) * high)
        for col in range(blocks):
            cols = slice(col * wide, (col + 1) * wide)
            block = out_ref[:, rows_at, cols]
            keep = mask_ref[tick, 0, k, col] != 0
            out_ref[:, rows_at, cols] = jnp.where(keep, block, jnp.zeros_like(block))


def masked_factor(block_mask, coupling, tick):
    rows, width = coupling.shape[3:]
    return pl.pallas_call(
        functools.partial(mask_body, tick=tick),
        grid_spec=pltpu.PrefetchScalarGridSpec(
            num_scalar_prefetch=1,
            grid=(1,),
            in_specs=[HBM],
            out_specs=VMEM,
            scratch_shapes=[pltpu.SemaphoreType.DMA((block_mask.shape[2],))],
        ),
        out_shape=jax.ShapeDtypeStruct((2, rows, width), BF16),
        compiler_params=LIMIT,
    )(block_mask, coupling)


def dot(a, b):
    return jnp.dot(a, b, preferred_element_type=F32)


def dot_t(a, b):
    return lax.dot_general(a, b, (((1,), (1,)), ((), ())), preferred_element_type=F32)


def fold_body(*refs, pieces, tick, start, first, last, chunks):
    mine, pidx, pw, here = refs[:4]
    refs = refs[4:]
    own = refs[0]
    factor = refs[1 : 1 + pieces]
    behind = refs[1 + pieces : 1 + 2 * pieces]
    before = refs[1 + 2 * pieces]
    right, low, high = refs[-3:]
    outs = refs[2 + 2 * pieces : -3]
    rows = own.shape[1]
    span = behind[0].shape[2]
    if first:
        green, sem = outs[-2:]
        outs = outs[:-2]
        fetch = pltpu.make_async_copy(before.at[tick, 0], green, sem)
        fetch.start()
    cols = slice(start, start + span)
    for k in range(pieces):
        size = behind[k].shape[1]
        at = slice(0, size)
        if pieces == 2:
            at = pl.ds(pl.multiple_of((mine[0] if k == 0 else 1 - mine[0]) * size, size), size)
        right[at, :span] = behind[k][0]
        right[at, span:] = behind[k][1]
        low[at, :span] = factor[k][0, :, cols]
        low[at, span:] = -factor[k][1, :, cols]
        high[at, :span] = factor[k][1, :, cols]
        high[at, span:] = factor[k][0, :, cols]
    tile = min(rows, 256)
    for step in range(rows // tile):
        at = slice(step * tile, (step + 1) * tile)
        a = dot(own[0, at], right[...])
        b = dot(own[1, at], right[...])
        half = jnp.concatenate([a[:, :span] - b[:, span:], a[:, span:] + b[:, :span]], axis=1).astype(BF16)
        real = dot_t(half, low[...])
        imag = dot_t(half, high[...])
        if first:
            if step == 0:
                fetch.wait()
            real = green[0, at].astype(F32) + real
            imag = green[1, at].astype(F32) + imag
        else:
            real = before[0, at] + real
            imag = before[1, at] + imag
        if not last:
            outs[0][0, at] = real
            outs[0][1, at] = imag
            continue
        real = real.astype(BF16)
        imag = imag.astype(BF16)
        left = 0
        for out in outs[:chunks]:
            out[0, at] = real[:, left : left + out.shape[2]]
            out[1, at] = imag[:, left : left + out.shape[2]]
            left += out.shape[2]
        if len(outs) > chunks:
            write_term(real, imag, pidx, pw, here, tick, outs[chunks:], step * tile)


def write_term(real, imag, pidx, pw, here, tick, outs, row):
    real = real.astype(F32)
    imag = imag.astype(F32)
    w0 = pw[0, pidx[0, 0, tick]]
    w1 = pw[1, pidx[0, 0, tick]]
    term_real = (w0 * real - w1 * imag).astype(BF16)
    term_imag = (w0 * imag + w1 * real).astype(BF16)
    high, width = real.shape
    if len(outs) == 1:
        outs[0][0, row : row + high] = term_real
        outs[0][1, row : row + high] = term_imag
        return
    part = row // outs[0].shape[0]
    row -= part * outs[0].shape[0]
    at = slice(row, row + high)
    real_send, real_keep, imag_send, imag_keep = outs[4 * part : 4 * part + 4]
    quarter = width // 4
    first_major = here[0] // 2 == 0
    first_minor = here[0] % 2 == 0
    lower, upper = term_real[:, : 2 * quarter], term_real[:, 2 * quarter :]
    real_send[at] = jnp.where(first_major, upper, lower)
    real_keep[at] = jnp.where(first_major, lower, upper)
    for pair in range(2):
        cols = slice(pair * quarter, (pair + 1) * quarter)
        even = term_imag[:, 2 * pair * quarter : (2 * pair + 1) * quarter]
        odd = term_imag[:, (2 * pair + 1) * quarter : (2 * pair + 2) * quarter]
        imag_send[at, cols] = jnp.where(first_minor, odd, even)
        imag_keep[at, cols] = jnp.where(first_minor, even, odd)


def term_shapes(rows, width):
    if lax.axis_size("pole") != 4:
        return [jax.ShapeDtypeStruct((2, rows, width), BF16)]
    parts = 2 if rows % 512 == 0 else 1
    return [jax.ShapeDtypeStruct((rows // parts, width // 2), BF16)] * (4 * parts)


def fold(scalars, own, factor, behind, before, tick, start, first, last, widths, with_term):
    rows, width = own.shape[1:]
    span = behind[0].shape[2]
    pieces = len(behind)
    if last:
        out_shape = [jax.ShapeDtypeStruct((2, rows, w), BF16) for w in widths]
        if with_term:
            out_shape += term_shapes(rows, width)
    else:
        out_shape = [jax.ShapeDtypeStruct((2, rows, width), F32)]
    scratch = [pltpu.VMEM((2, rows, width), BF16), pltpu.SemaphoreType.DMA] if first else []
    return pl.pallas_call(
        functools.partial(
            fold_body, pieces=pieces, tick=tick, start=start, first=first, last=last, chunks=len(widths)
        ),
        grid_spec=pltpu.PrefetchScalarGridSpec(
            num_scalar_prefetch=len(scalars),
            grid=(1,),
            in_specs=[VMEM] * (1 + 2 * pieces) + [HBM if first else VMEM],
            out_specs=[VMEM] * len(out_shape),
            scratch_shapes=scratch + [pltpu.VMEM((width, 2 * span), BF16)] * 3,
        ),
        out_shape=out_shape,
        input_output_aliases={} if first or last else {len(scalars) + 1 + 2 * pieces: 0},
        compiler_params=LIMIT,
    )(*scalars, own, *factor, *behind, before)


def term_body(pidx, pw, here, *refs, tick, count):
    rows = refs[0].shape[1]
    tile = min(rows, 256)
    for row in range(0, rows, tile):
        real = jnp.concatenate([ref[0, row : row + tile] for ref in refs[:count]], axis=1)
        imag = jnp.concatenate([ref[1, row : row + tile] for ref in refs[:count]], axis=1)
        write_term(real, imag, pidx, pw, here, tick, refs[count:], row)


def weigh(scalars, state, tick):
    out_shape = term_shapes(state[0].shape[1], sum(piece.shape[2] for piece in state))
    return pl.pallas_call(
        functools.partial(term_body, tick=tick, count=len(state)),
        grid_spec=pltpu.PrefetchScalarGridSpec(
            num_scalar_prefetch=3,
            grid=(1,),
            in_specs=[VMEM] * len(state),
            out_specs=[VMEM] * len(out_shape),
        ),
        out_shape=out_shape,
        compiler_params=LIMIT,
    )(*scalars[1:], *state)


def cut_body(mine, here, src, out, sem, *, start):
    fetch = pltpu.make_async_copy(src.at[0, :, :, pl.ds(start, out.shape[2])], out, sem)
    fetch.start()
    fetch.wait()


def cut_piece(mine, here, state, start, span):
    return pl.pallas_call(
        functools.partial(cut_body, start=start),
        grid_spec=pltpu.PrefetchScalarGridSpec(
            num_scalar_prefetch=2,
            grid=(1,),
            in_specs=[HBM],
            out_specs=VMEM,
            scratch_shapes=[pltpu.SemaphoreType.DMA],
        ),
        out_shape=jax.ShapeDtypeStruct((2, state.shape[2], span), BF16),
        compiler_params=LIMIT,
    )(mine, here, state)


def picked(ref, which):
    quarter = ref.shape[1] // 2
    return jnp.where(which == 0, ref[:, :quarter], ref[:, quarter:]).astype(F32)


def pass_on_body(here, real_keep, real_got, imag_keep, imag_got, real_send, imag_send):
    major, minor = here[0] // 2, here[0] % 2
    real_send[...] = (picked(real_keep, 1 - minor) + picked(real_got, 1 - minor)).astype(BF16)
    imag_send[...] = (picked(imag_keep, 1 - major) + picked(imag_got, 1 - major)).astype(BF16)


def retain_body(here, *refs, parts, extra):
    major, minor = here[0] // 2, here[0] % 2
    out = refs[-1]
    high = refs[0].shape[0]
    for k in range(parts):
        real_keep, real_got, imag_keep, imag_got = refs[4 * k : 4 * k + 4]
        at = slice(k * high, (k + 1) * high)
        real = picked(real_keep, minor) + picked(real_got, minor)
        imag = picked(imag_keep, major) + picked(imag_got, major)
        if extra:
            real = refs[4 * parts][0, at] + real
            imag = refs[4 * parts][1, at] + imag
        out[0, at] = real
        out[1, at] = imag


def close_body(base, *refs):
    out = refs[-1]
    parts = len(refs) // 2
    high = refs[0].shape[0]
    for k in range(parts):
        at = slice(k * high, (k + 1) * high)
        out[0, at] = base[0, at] + refs[2 * k][...].astype(F32)
        out[1, at] = base[1, at] + refs[2 * k + 1][...].astype(F32)


def kernel_call(fn, scalars, args, out_shape):
    many = isinstance(out_shape, list)
    return pl.pallas_call(
        fn,
        grid_spec=pltpu.PrefetchScalarGridSpec(
            num_scalar_prefetch=len(scalars),
            grid=(1,),
            in_specs=[VMEM] * len(args),
            out_specs=[VMEM] * len(out_shape) if many else VMEM,
        ),
        out_shape=out_shape,
        compiler_params=LIMIT,
    )(*scalars, *args)


def scatter_sum(terms, before, here):
    if len(terms) == 1:
        share = lax.psum_scatter(terms[0], "pole", scatter_dimension=2, tiled=True).astype(F32)
        return share if before is None else before + share
    parts = len(terms) // 4
    high, half = terms[0].shape
    quarter = half // 2
    fields = []
    for k in range(parts):
        real_out, real_keep, imag_out, imag_keep = terms[4 * k : 4 * k + 4]
        real_got = flip(real_out, "pole", 2)
        imag_got = flip(imag_out, "pole", 1)
        fields.append((real_keep, real_got, imag_keep, imag_got))
    lasts = []
    for k in range(parts):
        sends = kernel_call(
            pass_on_body, (here,), fields[k], [jax.ShapeDtypeStruct((high, quarter), BF16)] * 2
        )
        lasts.append(flip(sends[0], "pole", 1))
        lasts.append(flip(sends[1], "pole", 2))
    extra = [] if before is None else [before]
    shape = jax.ShapeDtypeStruct((2, parts * high, quarter), F32)
    flat = [value for field in fields for value in field]
    retain = functools.partial(retain_body, parts=parts, extra=len(extra))
    base = kernel_call(retain, (here,), flat + extra, shape)
    return kernel_call(close_body, (), [base, *lasts], shape)


def spans(width):
    unit = width // 8
    if unit % 128:
        return [width]
    return [3 * unit, 2 * unit, 2 * unit, unit]


def body(local_green, coupling, block_mask, state_in, pole_weight, pole_index):
    local_green, coupling, state_in = (
        pltpu.with_memory_space_constraint(value, pltpu.HBM) for value in (local_green, coupling, state_in)
    )
    ticks = coupling.shape[0]
    width = coupling.shape[4]
    sizes = spans(width)
    starts = [sum(sizes[:c]) for c in range(len(sizes))]
    here = jnp.reshape(lax.axis_index("pole").astype(jnp.int32), (1,))
    mine = jnp.reshape(lax.axis_index("row").astype(jnp.int32), (1,))
    scalars = (mine, jnp.transpose(pole_index, (1, 2, 0)), pole_weight, here)
    state = []
    for c, start in enumerate(starts):
        state.append(cut_piece(mine, here, state_in, start, sizes[c]))
    owns = []
    factors = []
    density = None
    for tick in range(ticks):
        own = masked_factor(block_mask, coupling, tick)
        owns.append(own)
        factors.append(row_pieces(own))
    for tick in range(ticks):
        incoming = []
        for c in range(len(sizes)):
            incoming.append(from_behind(state[c], "slab"))
        own, factor = owns[tick], factors[tick]
        before = local_green
        last_tick = tick == ticks - 1
        widths = [width] if last_tick else sizes
        for c, start in enumerate(starts):
            behind = row_pieces(incoming[c])
            last = c == len(sizes) - 1
            outs = fold(
                scalars, own, factor, behind, before, tick, start, c == 0, last, widths if last else [], last_tick
            )
            before = outs[0]
        state = outs[: len(widths)]
        terms = outs[len(widths) :] or weigh(scalars, state, tick)
        density = scatter_sum(terms, density, here)
    return (state[0][None], density)


def solution(mesh):
    placed = (
        P(None, "pole", None, ("slab", "row"), None),
        P(None, "pole", None, ("slab", "row"), None),
        P(None, "pole", ("slab", "row"), None),
        P("pole", None, ("slab", "row"), None),
        P(),
        P(None, "pole", "slab"),
    )
    return jax.shard_map(
        body,
        mesh=mesh,
        in_specs=placed,
        out_specs=(P("pole", None, ("slab", "row"), None), P(None, ("slab", "row"), "pole")),
        check_vma=False,
    )
```

```python
import functools

import jax
import jax.numpy as jnp
from jax import lax
from jax.experimental import pallas as pl
from jax.experimental.pallas import tpu as pltpu
from jax.sharding import PartitionSpec as P


BF16 = jnp.bfloat16
F32 = jnp.float32

LIMIT = pltpu.CompilerParams(vmem_limit_bytes=20 << 20)


def shift(block, axis, step):
    devices = range(lax.axis_size(axis))
    return lax.ppermute(block, axis, [(i, i + step) for i in devices if i + step in devices])


def flip(block, axis, bit):
    return lax.ppermute(block, axis, [(i, i ^ bit) for i in range(lax.axis_size(axis))])


def row_pieces(block, dim=1):
    count = lax.axis_size("row")
    if count == 1:
        return [block]
    if count == 2:
        there = flip(block, "row", 1)
        return [block, there]
    return [lax.all_gather(block, "row", axis=dim, tiled=True)]


VMEM = pl.BlockSpec(memory_space=pltpu.VMEM)
HBM = pl.BlockSpec(memory_space=pltpu.HBM)


def mask_body(mask_ref, coupling_ref, out_ref, sems, *, tick):
    block_rows, blocks = mask_ref.shape[2:]
    rows, width = out_ref.shape[1:]
    high, wide = rows // block_rows, width // blocks

    def fetch(k):
        at = pl.ds(k * high, high)
        return pltpu.make_async_copy(coupling_ref.at[tick, 0, :, at, :], out_ref.at[:, at, :], sems.at[k])

    for k in range(block_rows):
        fetch(k).start()
    for k in range(block_rows):
        fetch(k).wait()
        rows_at = slice(k * high, (k + 1) * high)
        for col in range(blocks):
            cols = slice(col * wide, (col + 1) * wide)
            block = out_ref[:, rows_at, cols]
            keep = mask_ref[tick, 0, k, col] != 0
            out_ref[:, rows_at, cols] = jnp.where(keep, block, jnp.zeros_like(block))


def masked_factor(block_mask, coupling, tick):
    rows, width = coupling.shape[3:]
    return pl.pallas_call(
        functools.partial(mask_body, tick=tick),
        grid_spec=pltpu.PrefetchScalarGridSpec(
            num_scalar_prefetch=1,
            grid=(1,),
            in_specs=[HBM],
            out_specs=VMEM,
            scratch_shapes=[pltpu.SemaphoreType.DMA((block_mask.shape[2],))],
        ),
        out_shape=jax.ShapeDtypeStruct((2, rows, width), BF16),
        compiler_params=LIMIT,
    )(block_mask, coupling)


def dot(a, b):
    return jnp.dot(a, b, preferred_element_type=F32)


def dot_t(a, b):
    return lax.dot_general(a, b, (((1,), (1,)), ((), ())), preferred_element_type=F32)


def plan_body(mine, *refs, tick):
    out = refs[-1]
    masks = refs[:-1]
    blocks = masks[0].shape[3]
    rows = []
    for j in range(blocks):
        bits = jnp.int32(0)
        for c in range(blocks):
            if len(masks) == 1:
                value = masks[0][tick, 0, j, c]
            else:
                half = blocks // 2
                a = masks[0][tick, 0, j % half, c]
                b = masks[1][tick, 0, j % half, c]
                value = jnp.where(mine[0] == j // half, a, b)
            bits = bits + jnp.where(value != 0, jnp.int32(1 << c), jnp.int32(0))
        rows.append(bits)
    best = jnp.int32(-1)
    pair = jnp.int32(0)
    for c in range(1, blocks):
        for d in range(c + 1, blocks):
            count = jnp.int32(0)
            for bits in rows:
                count = count + jnp.where((bits & ((1 << c) | (1 << d))) == 0, jnp.int32(1), jnp.int32(0))
            pair = jnp.where(count > best, jnp.int32((1 << c) | (1 << d)), pair)
            best = jnp.maximum(best, count)
    soon = jnp.int32(0)
    late = jnp.int32(blocks - 2)
    for c in range(blocks):
        is_late = (pair & (1 << c)) != 0
        out[jnp.where(is_late, late, soon)] = jnp.int32(c)
        step = jnp.where(is_late, jnp.int32(1), jnp.int32(0))
        late = late + step
        soon = soon + 1 - step
    lead = jnp.int32(0)
    rest = jnp.int32(2)
    for j in range(blocks):
        leads = jnp.logical_and((rows[j] & pair) == 0, lead < 2)
        at = jnp.where(leads, lead, jnp.minimum(rest, blocks - 1))
        out[blocks + at] = jnp.int32(j)
        step = jnp.where(leads, jnp.int32(1), jnp.int32(0))
        lead = lead + step
        rest = rest + 1 - step


def make_plan(mine, masks, tick):
    blocks = masks[0].shape[3]
    smem = pl.BlockSpec(memory_space=pltpu.SMEM)
    return pl.pallas_call(
        functools.partial(plan_body, tick=tick),
        grid_spec=pltpu.PrefetchScalarGridSpec(
            num_scalar_prefetch=1, grid=(1,), in_specs=[smem] * len(masks), out_specs=smem
        ),
        out_shape=jax.ShapeDtypeStruct((2 * blocks,), jnp.int32),
        compiler_params=LIMIT,
        name="plan",
    )(mine, *masks)


def cut_body(mine, here, plan, src, out, sems, *, first, blocks):
    wide = src.shape[3] // blocks
    copies = []
    for u in range(out.shape[2] // wide):
        at = slice(0, wide) if first is None else pl.ds(pl.multiple_of(plan[first + u] * wide, wide), wide)
        to = slice(u * wide, (u + 1) * wide)
        copies.append(pltpu.make_async_copy(src.at[0, :, :, at], out.at[:, :, to], sems.at[u]))
    for copy in copies:
        copy.start()
    for copy in copies:
        copy.wait()


def cut_piece(mine, here, plan, state, first, units, blocks):
    rows, width = state.shape[2:]
    return pl.pallas_call(
        functools.partial(cut_body, first=first, blocks=blocks),
        grid_spec=pltpu.PrefetchScalarGridSpec(
            num_scalar_prefetch=3,
            grid=(1,),
            in_specs=[HBM],
            out_specs=VMEM,
            scratch_shapes=[pltpu.SemaphoreType.DMA((units,))],
        ),
        out_shape=jax.ShapeDtypeStruct((2, rows, units * width // blocks), BF16),
        compiler_params=LIMIT,
    )(mine, here, plan, state)


def fold_body(*refs, pieces, tick, first, kind, base, top, count, blocks):
    mine, pidx, pw, here, plan = refs[:5]
    own = refs[5]
    refs = refs[6:]
    factor = refs[:pieces]
    behind = refs[pieces : 2 * pieces]
    before = refs[2 * pieces]
    right, low, high = refs[-3:]
    outs = refs[1 + 2 * pieces : -3]
    span = behind[0].shape[2]
    wide = own.shape[2] // blocks

    def block_cols(index):
        return pl.ds(pl.multiple_of(plan[index] * wide, wide), wide)

    if first:
        green, sem = outs[-2:]
        outs = outs[:-2]
        fetch = pltpu.make_async_copy(before.at[tick, 0], green, sem)
        fetch.start()
    for k in range(pieces):
        size = behind[k].shape[1]
        at = slice(0, size)
        if pieces == 2:
            at = pl.ds(pl.multiple_of((mine[0] if k == 0 else 1 - mine[0]) * size, size), size)
        right[at, :span] = behind[k][0]
        right[at, span:] = behind[k][1]
        for u in range(span // wide):
            cols = block_cols(base + u)
            real = factor[k][0, :, cols]
            imag = factor[k][1, :, cols]
            one = slice(u * wide, (u + 1) * wide)
            two = slice(span + u * wide, span + (u + 1) * wide)
            low[at, one] = real
            low[at, two] = -imag
            high[at, one] = imag
            high[at, two] = real
    tile = min(count, 256)
    for step in range(count // tile):
        at = slice(top + step * tile, top + (step + 1) * tile)
        to = slice(step * tile, (step + 1) * tile)
        a = dot(own[0, at], right[...])
        b = dot(own[1, at], right[...])
        half = jnp.concatenate([a[:, :span] - b[:, span:], a[:, span:] + b[:, :span]], axis=1).astype(BF16)
        real = dot_t(half, low[...])
        imag = dot_t(half, high[...])
        if first:
            if step == 0:
                fetch.wait()
            real = green[0, at].astype(F32) + real
            imag = green[1, at].astype(F32) + imag
        else:
            real = before[0, at] + real
            imag = before[1, at] + imag
        outs[0][0, to] = real.astype(outs[0].dtype)
        outs[0][1, to] = imag.astype(outs[0].dtype)
        if kind == "final":
            write_term(real.astype(BF16), imag.astype(BF16), pidx, pw, here, tick, outs[1:], step * tile)
            continue
        index = blocks if kind == "lead" else blocks + 2
        for out in outs[1:]:
            for u in range(out.shape[2] // wide):
                for part in range(2):
                    out[part, to, u * wide : (u + 1) * wide] = outs[0][part, to, block_cols(index)].astype(BF16)
                index += 1


def write_term(real, imag, pidx, pw, here, tick, outs, row):
    real = real.astype(F32)
    imag = imag.astype(F32)
    w0 = pw[0, pidx[0, 0, tick]]
    w1 = pw[1, pidx[0, 0, tick]]
    term_real = (w0 * real - w1 * imag).astype(BF16)
    term_imag = (w0 * imag + w1 * real).astype(BF16)
    high, width = real.shape
    if len(outs) == 1:
        outs[0][0, row : row + high] = term_real
        outs[0][1, row : row + high] = term_imag
        return
    part = row // outs[0].shape[0]
    row -= part * outs[0].shape[0]
    at = slice(row, row + high)
    real_send, real_keep, imag_send, imag_keep = outs[4 * part : 4 * part + 4]
    quarter = width // 4
    first_major = here[0] // 2 == 0
    first_minor = here[0] % 2 == 0
    lower, upper = term_real[:, : 2 * quarter], term_real[:, 2 * quarter :]
    real_send[at] = jnp.where(first_major, upper, lower)
    real_keep[at] = jnp.where(first_major, lower, upper)
    for pair in range(2):
        cols = slice(pair * quarter, (pair + 1) * quarter)
        even = term_imag[:, 2 * pair * quarter : (2 * pair + 1) * quarter]
        odd = term_imag[:, (2 * pair + 1) * quarter : (2 * pair + 2) * quarter]
        imag_send[at, cols] = jnp.where(first_minor, odd, even)
        imag_keep[at, cols] = jnp.where(first_minor, even, odd)


def term_shapes(rows, width):
    if lax.axis_size("pole") != 4:
        return [jax.ShapeDtypeStruct((2, rows, width), BF16)]
    parts = 2 if rows % 512 == 0 else 1
    return [jax.ShapeDtypeStruct((rows // parts, width // 2), BF16)] * (4 * parts)


def fold(scalars, own, factor, behind, before, tick, first, kind, base, sends=(), part=None):
    rows, width = own.shape[1:]
    blocks = scalars[4].shape[0] // 2
    wide = width // blocks
    span = behind[0].shape[2]
    pieces = len(behind)
    top, count = (0, rows) if part is None else (part[0] * (rows // part[1]), rows // part[1])
    done = kind in ("final", "send")
    out_shape = [jax.ShapeDtypeStruct((2, count, width), BF16 if done else F32)]
    out_shape += [jax.ShapeDtypeStruct((2, rows, units * wide), BF16) for units in sends]
    if kind == "final":
        out_shape += term_shapes(rows, width)[: 4 if part[1] == 2 else None]
    scratch = [pltpu.VMEM((2, rows, width), BF16), pltpu.SemaphoreType.DMA] if first else []
    body = functools.partial(
        fold_body, pieces=pieces, tick=tick, first=first, kind=kind, base=base, top=top, count=count, blocks=blocks
    )
    return pl.pallas_call(
        body,
        grid_spec=pltpu.PrefetchScalarGridSpec(
            num_scalar_prefetch=len(scalars),
            grid=(1,),
            in_specs=[VMEM] * (1 + 2 * pieces) + [HBM if first else VMEM],
            out_specs=[VMEM] * len(out_shape),
            scratch_shapes=scratch + [pltpu.VMEM((width, 2 * span), BF16)] * 3,
        ),
        out_shape=out_shape,
        input_output_aliases={} if first or done else {len(scalars) + 1 + 2 * pieces: 0},
        compiler_params=LIMIT,
    )(*scalars, own, *factor, *behind, before)


def term_body(pidx, pw, here, *refs, tick, count):
    rows = refs[0].shape[1]
    tile = min(rows, 256)
    for row in range(0, rows, tile):
        real = jnp.concatenate([ref[0, row : row + tile] for ref in refs[:count]], axis=1)
        imag = jnp.concatenate([ref[1, row : row + tile] for ref in refs[:count]], axis=1)
        write_term(real, imag, pidx, pw, here, tick, refs[count:], row)


def weigh(scalars, state, tick):
    out_shape = term_shapes(state[0].shape[1], sum(piece.shape[2] for piece in state))
    return pl.pallas_call(
        functools.partial(term_body, tick=tick, count=len(state)),
        grid_spec=pltpu.PrefetchScalarGridSpec(
            num_scalar_prefetch=3,
            grid=(1,),
            in_specs=[VMEM] * len(state),
            out_specs=[VMEM] * len(out_shape),
        ),
        out_shape=out_shape,
        compiler_params=LIMIT,
    )(*scalars[1:], *state)


def emit_body(*refs):
    out, sems = refs[-2:]
    parts = refs[:-2]
    high = parts[0].shape[1]
    copies = [
        pltpu.make_async_copy(ref, out.at[0, :, pl.ds(k * high, high), :], sems.at[k]) for k, ref in enumerate(parts)
    ]
    for copy in copies:
        copy.start()
    for copy in copies:
        copy.wait()


def emit(parts):
    high, width = parts[0].shape[1:]
    return pl.pallas_call(
        emit_body,
        in_specs=[VMEM] * len(parts),
        out_specs=HBM,
        out_shape=jax.ShapeDtypeStruct((1, 2, high * len(parts), width), BF16),
        scratch_shapes=[pltpu.SemaphoreType.DMA((len(parts),))],
        compiler_params=LIMIT,
        name="emit",
    )(*parts)


def picked(ref, which):
    quarter = ref.shape[1] // 2
    return jnp.where(which == 0, ref[:, :quarter], ref[:, quarter:]).astype(F32)


def pass_on_body(here, real_keep, real_got, imag_keep, imag_got, real_send, imag_send):
    major, minor = here[0] // 2, here[0] % 2
    real_send[...] = (picked(real_keep, 1 - minor) + picked(real_got, 1 - minor)).astype(BF16)
    imag_send[...] = (picked(imag_keep, 1 - major) + picked(imag_got, 1 - major)).astype(BF16)


def retain_body(here, *refs, parts, extra):
    major, minor = here[0] // 2, here[0] % 2
    out = refs[-1]
    high = refs[0].shape[0]
    for k in range(parts):
        real_keep, real_got, imag_keep, imag_got = refs[4 * k : 4 * k + 4]
        at = slice(k * high, (k + 1) * high)
        real = picked(real_keep, minor) + picked(real_got, minor)
        imag = picked(imag_keep, major) + picked(imag_got, major)
        if extra:
            real = refs[4 * parts][0, at] + real
            imag = refs[4 * parts][1, at] + imag
        out[0, at] = real
        out[1, at] = imag


def close_body(base, *refs):
    out = refs[-1]
    parts = len(refs) // 2
    high = refs[0].shape[0]
    for k in range(parts):
        at = slice(k * high, (k + 1) * high)
        out[0, at] = base[0, at] + refs[2 * k][...].astype(F32)
        out[1, at] = base[1, at] + refs[2 * k + 1][...].astype(F32)


def kernel_call(fn, scalars, args, out_shape):
    many = isinstance(out_shape, list)
    return pl.pallas_call(
        fn,
        grid_spec=pltpu.PrefetchScalarGridSpec(
            num_scalar_prefetch=len(scalars),
            grid=(1,),
            in_specs=[VMEM] * len(args),
            out_specs=[VMEM] * len(out_shape) if many else VMEM,
        ),
        out_shape=out_shape,
        compiler_params=LIMIT,
    )(*scalars, *args)


def scatter_sum(terms, before, here):
    if len(terms) == 1:
        share = lax.psum_scatter(terms[0], "pole", scatter_dimension=2, tiled=True).astype(F32)
        return share if before is None else before + share
    parts = len(terms) // 4
    high, half = terms[0].shape
    quarter = half // 2
    fields = []
    for k in range(parts):
        real_out, real_keep, imag_out, imag_keep = terms[4 * k : 4 * k + 4]
        real_got = flip(real_out, "pole", 2)
        imag_got = flip(imag_out, "pole", 1)
        fields.append((real_keep, real_got, imag_keep, imag_got))
    lasts = []
    for k in range(parts):
        sends = kernel_call(pass_on_body, (here,), fields[k], [jax.ShapeDtypeStruct((high, quarter), BF16)] * 2)
        lasts.append(flip(sends[0], "pole", 1))
        lasts.append(flip(sends[1], "pole", 2))
    extra = [] if before is None else [before]
    shape = jax.ShapeDtypeStruct((2, parts * high, quarter), F32)
    flat = [value for field in fields for value in field]
    retain = functools.partial(retain_body, parts=parts, extra=len(extra))
    base = kernel_call(retain, (here,), flat + extra, shape)
    return kernel_call(close_body, (), [base, *lasts], shape)


ARRIVE = (1, 3, 2, 2)
LEAVE = (2, 3, 2, 1)


def body(local_green, coupling, block_mask, state_in, pole_weight, pole_index):
    local_green, coupling, state_in = (
        pltpu.with_memory_space_constraint(value, pltpu.HBM) for value in (local_green, coupling, state_in)
    )
    ticks = coupling.shape[0]
    blocks = block_mask.shape[3]
    here = jnp.reshape(lax.axis_index("pole").astype(jnp.int32), (1,))
    mine = jnp.reshape(lax.axis_index("row").astype(jnp.int32), (1,))
    masks = row_pieces(block_mask, 2)
    state = [cut_piece(mine, here, mine, state_in, None, 1, blocks)]
    plan = make_plan(mine, masks, 0)
    plan_up = shift(plan, "slab", 1)
    plan_down = shift(plan, "slab", -1)
    at = 1
    for units in ARRIVE[1:]:
        state.append(cut_piece(mine, here, plan_up, state_in, at, units, blocks))
        at += units
    owns = []
    factors = []
    for tick in range(ticks):
        own = masked_factor(block_mask, coupling, tick)
        owns.append(own)
        factors.append(row_pieces(own))
    weights = (mine, jnp.transpose(pole_index, (1, 2, 0)), pole_weight, here)
    density = None
    incoming = []
    for piece in state:
        incoming.append(shift(piece, "slab", -1))
    for tick in range(ticks):
        own, factor = owns[tick], factors[tick]
        scalars = (*weights, plan_down if tick else plan)
        base = blocks if tick else 0
        before = local_green
        last_tick = tick == ticks - 1
        leaving = []
        for c, piece in enumerate(incoming):
            behind = row_pieces(piece)
            last = c == len(incoming) - 1
            kind, sends = "sum", ()
            if not last_tick and c == len(incoming) - 2:
                kind, sends = "lead", LEAVE[:1]
            if not last_tick and last:
                kind, sends = "send", LEAVE[1:]
            if last_tick and last:
                break
            outs = fold(scalars, own, factor, behind, before, tick, c == 0, kind, base, sends)
            before = outs[0]
            base += piece.shape[2] * blocks // own.shape[2]
            for block in outs[1:]:
                leaving.append(shift(block, "slab", -1))
        if last_tick:
            shapes = len(term_shapes(*own.shape[1:]))
            parts = 2 if shapes == 8 else 1
            finals = []
            terms = []
            for k in range(parts):
                outs = fold(scalars, own, factor, behind, before, tick, False, "final", base, (), (k, parts))
                finals.append(outs[0])
                terms += outs[1:]
            density = scatter_sum(terms, density, here)
            state_out = emit(finals)
        else:
            terms = weigh(scalars[:4], [before], tick)
            density = scatter_sum(terms, density, here)
        incoming = leaving
    return (state_out, density)


def solution(mesh):
    placed = (
        P(None, "pole", None, ("slab", "row"), None),
        P(None, "pole", None, ("slab", "row"), None),
        P(None, "pole", ("slab", "row"), None),
        P("pole", None, ("slab", "row"), None),
        P(),
        P(None, "pole", "slab"),
    )
    return jax.shard_map(
        body,
        mesh=mesh,
        in_specs=placed,
        out_specs=(P("pole", None, ("slab", "row"), None), P(None, ("slab", "row"), "pole")),
        check_vma=False,
    )
```

```python
import functools

import jax
import jax.numpy as jnp
from jax import lax
from jax.experimental import pallas as pl
from jax.experimental.pallas import tpu as pltpu
from jax.sharding import PartitionSpec as P


BF16 = jnp.bfloat16
F32 = jnp.float32

LIMIT = pltpu.CompilerParams(vmem_limit_bytes=20 << 20)


def shift(block, axis, step):
    devices = range(lax.axis_size(axis))
    return lax.ppermute(block, axis, [(i, i + step) for i in devices if i + step in devices])


def flip(block, axis, bit):
    return lax.ppermute(block, axis, [(i, i ^ bit) for i in range(lax.axis_size(axis))])


def row_pieces(block, dim=1):
    count = lax.axis_size("row")
    if count == 1:
        return [block]
    if count == 2:
        there = flip(block, "row", 1)
        return [block, there]
    return [lax.all_gather(block, "row", axis=dim, tiled=True)]


VMEM = pl.BlockSpec(memory_space=pltpu.VMEM)
HBM = pl.BlockSpec(memory_space=pltpu.HBM)


def mask_body(mask_ref, coupling_ref, out_ref, sems, *, tick):
    block_rows, blocks = mask_ref.shape[2:]
    rows, width = out_ref.shape[1:]
    high, wide = rows // block_rows, width // blocks

    def fetch(k):
        at = pl.ds(k * high, high)
        return pltpu.make_async_copy(coupling_ref.at[tick, 0, :, at, :], out_ref.at[:, at, :], sems.at[k])

    for k in range(block_rows):
        fetch(k).start()
    for k in range(block_rows):
        fetch(k).wait()
        rows_at = slice(k * high, (k + 1) * high)
        for col in range(blocks):
            cols = slice(col * wide, (col + 1) * wide)
            block = out_ref[:, rows_at, cols]
            keep = mask_ref[tick, 0, k, col] != 0
            out_ref[:, rows_at, cols] = jnp.where(keep, block, jnp.zeros_like(block))


def masked_factor(block_mask, coupling, tick):
    rows, width = coupling.shape[3:]
    return pl.pallas_call(
        functools.partial(mask_body, tick=tick),
        grid_spec=pltpu.PrefetchScalarGridSpec(
            num_scalar_prefetch=1,
            grid=(1,),
            in_specs=[HBM],
            out_specs=VMEM,
            scratch_shapes=[pltpu.SemaphoreType.DMA((block_mask.shape[2],))],
        ),
        out_shape=jax.ShapeDtypeStruct((2, rows, width), BF16),
        compiler_params=LIMIT,
    )(block_mask, coupling)


def dot(a, b):
    return jnp.dot(a, b, preferred_element_type=F32)


def dot_t(a, b):
    return lax.dot_general(a, b, (((1,), (1,)), ((), ())), preferred_element_type=F32)


def plan_body(mine, *refs, tick):
    out = refs[-1]
    masks = refs[:-1]
    blocks = masks[0].shape[3]
    one, none = jnp.int32(1), jnp.int32(0)
    rows = []
    for j in range(blocks):
        bits = none
        for c in range(blocks):
            if len(masks) == 1:
                value = masks[0][tick, 0, j, c]
            else:
                half = blocks // 2
                a = masks[0][tick, 0, j % half, c]
                b = masks[1][tick, 0, j % half, c]
                value = jnp.where(mine[0] == j // half, a, b)
            bits = bits + jnp.where(value != 0, jnp.int32(1 << c), none)
        rows.append(bits)

    def widest(start):
        best, found = jnp.int32(-1), none
        for c in range(2, blocks):
            both = start | (1 << c)
            count = none
            for bits in rows:
                count = count + jnp.where((bits & both) == 0, one, none)
            count = jnp.where((start & (1 << c)) != 0, jnp.int32(-1), count)
            found = jnp.where(count > best, jnp.int32(1 << c), found)
            best = jnp.maximum(best, count)
        return found

    last = widest(none)
    near = widest(last)
    soon = none
    for c in range(blocks):
        is_last = (last & (1 << c)) != 0
        is_near = (near & (1 << c)) != 0
        at = jnp.where(is_last, jnp.int32(blocks - 1), jnp.where(is_near, jnp.int32(blocks - 2), soon))
        out[at] = jnp.int32(c)
        soon = soon + jnp.where(jnp.logical_or(is_last, is_near), none, one)
    lead, next_two, rest = none, one, jnp.int32(3)
    for j in range(blocks):
        leads = jnp.logical_and((rows[j] & (last | near)) == 0, lead == 0)
        follows = jnp.logical_and((rows[j] & last) == 0, next_two < 3)
        follows = jnp.logical_and(follows, jnp.logical_not(leads))
        at = jnp.where(leads, none, jnp.where(follows, next_two, jnp.minimum(rest, blocks - 1)))
        out[blocks + at] = jnp.int32(j)
        lead = lead + jnp.where(leads, one, none)
        next_two = next_two + jnp.where(follows, one, none)
        rest = rest + jnp.where(jnp.logical_or(leads, follows), none, one)


def make_plan(mine, masks, tick):
    blocks = masks[0].shape[3]
    smem = pl.BlockSpec(memory_space=pltpu.SMEM)
    return pl.pallas_call(
        functools.partial(plan_body, tick=tick),
        grid_spec=pltpu.PrefetchScalarGridSpec(
            num_scalar_prefetch=1, grid=(1,), in_specs=[smem] * len(masks), out_specs=smem
        ),
        out_shape=jax.ShapeDtypeStruct((2 * blocks,), jnp.int32),
        compiler_params=LIMIT,
        name="plan",
    )(mine, *masks)


def cut_body(mine, here, plan, src, out, sems, *, first, blocks):
    wide = src.shape[3] // blocks if first else out.shape[2]
    copies = []
    for u in range(out.shape[2] // wide):
        at = pl.ds(pl.multiple_of(plan[first + u] * wide, wide) if first else 0, wide)
        to = slice(u * wide, (u + 1) * wide)
        copies.append(pltpu.make_async_copy(src.at[0, :, :, at], out.at[:, :, to], sems.at[u]))
    for copy in copies:
        copy.start()
    for copy in copies:
        copy.wait()


def cut_piece(mine, here, plan, state, first, units, blocks):
    rows, width = state.shape[2:]
    return pl.pallas_call(
        functools.partial(cut_body, first=first, blocks=blocks),
        grid_spec=pltpu.PrefetchScalarGridSpec(
            num_scalar_prefetch=3,
            grid=(1,),
            in_specs=[HBM],
            out_specs=VMEM,
            scratch_shapes=[pltpu.SemaphoreType.DMA((units,))],
        ),
        out_shape=jax.ShapeDtypeStruct((2, rows, units * width // blocks), BF16),
        compiler_params=LIMIT,
    )(mine, here, plan, state)


def fold_body(*refs, pieces, tick, first, kind, base, index, top, count, blocks):
    mine, pidx, pw, here, plan = refs[:5]
    own = refs[5]
    refs = refs[6:]
    factor = refs[:pieces]
    behind = refs[pieces : 2 * pieces]
    before = refs[2 * pieces]
    right, low, high = refs[-3:]
    outs = refs[1 + 2 * pieces : -3]
    span = behind[0].shape[2]
    wide = own.shape[2] // blocks

    def block_cols(index):
        return pl.ds(pl.multiple_of(plan[index] * wide, wide), wide)

    if first:
        green, sem = outs[-2:]
        outs = outs[:-2]
        fetch = pltpu.make_async_copy(before.at[tick, 0], green, sem)
        fetch.start()
    for k in range(pieces):
        size = behind[k].shape[1]
        at = slice(0, size)
        if pieces == 2:
            at = pl.ds(pl.multiple_of((mine[0] if k == 0 else 1 - mine[0]) * size, size), size)
        right[at, :span] = behind[k][0]
        right[at, span:] = behind[k][1]
        for u in range(span // wide):
            cols = block_cols(base + u)
            real = factor[k][0, :, cols]
            imag = factor[k][1, :, cols]
            one = slice(u * wide, (u + 1) * wide)
            two = slice(span + u * wide, span + (u + 1) * wide)
            low[at, one] = real
            low[at, two] = -imag
            high[at, one] = imag
            high[at, two] = real
    tile = min(count, 256)
    for step in range(count // tile):
        at = slice(top + step * tile, top + (step + 1) * tile)
        to = slice(step * tile, (step + 1) * tile)
        a = dot(own[0, at], right[...])
        b = dot(own[1, at], right[...])
        half = jnp.concatenate([a[:, :span] - b[:, span:], a[:, span:] + b[:, :span]], axis=1).astype(BF16)
        real = dot_t(half, low[...])
        imag = dot_t(half, high[...])
        if first:
            if step == 0:
                fetch.wait()
            real = green[0, at].astype(F32) + real
            imag = green[1, at].astype(F32) + imag
        else:
            real = before[0, at] + real
            imag = before[1, at] + imag
        outs[0][0, to] = real.astype(outs[0].dtype)
        outs[0][1, to] = imag.astype(outs[0].dtype)
        if kind == "final":
            write_term(real.astype(BF16), imag.astype(BF16), pidx, pw, here, tick, outs[1:], step * tile)
            continue
        at_block = blocks + index
        for out in outs[1:]:
            for u in range(out.shape[2] // wide):
                for part in range(2):
                    out[part, to, u * wide : (u + 1) * wide] = outs[0][part, to, block_cols(at_block)].astype(BF16)
                at_block += 1


def write_term(real, imag, pidx, pw, here, tick, outs, row):
    real = real.astype(F32)
    imag = imag.astype(F32)
    w0 = pw[0, pidx[0, 0, tick]]
    w1 = pw[1, pidx[0, 0, tick]]
    term_real = (w0 * real - w1 * imag).astype(BF16)
    term_imag = (w0 * imag + w1 * real).astype(BF16)
    high, width = real.shape
    if len(outs) == 1:
        outs[0][0, row : row + high] = term_real
        outs[0][1, row : row + high] = term_imag
        return
    part = row // outs[0].shape[0]
    row -= part * outs[0].shape[0]
    at = slice(row, row + high)
    real_send, real_keep, imag_send, imag_keep = outs[4 * part : 4 * part + 4]
    quarter = width // 4
    first_major = here[0] // 2 == 0
    first_minor = here[0] % 2 == 0
    lower, upper = term_real[:, : 2 * quarter], term_real[:, 2 * quarter :]
    real_send[at] = jnp.where(first_major, upper, lower)
    real_keep[at] = jnp.where(first_major, lower, upper)
    for pair in range(2):
        cols = slice(pair * quarter, (pair + 1) * quarter)
        even = term_imag[:, 2 * pair * quarter : (2 * pair + 1) * quarter]
        odd = term_imag[:, (2 * pair + 1) * quarter : (2 * pair + 2) * quarter]
        imag_send[at, cols] = jnp.where(first_minor, odd, even)
        imag_keep[at, cols] = jnp.where(first_minor, even, odd)


def term_shapes(rows, width):
    if lax.axis_size("pole") != 4:
        return [jax.ShapeDtypeStruct((2, rows, width), BF16)]
    parts = 2 if rows % 512 == 0 else 1
    return [jax.ShapeDtypeStruct((rows // parts, width // 2), BF16)] * (4 * parts)


def fold(scalars, own, factor, behind, before, tick, first, kind, base, sends=(), index=0, part=None):
    rows, width = own.shape[1:]
    blocks = scalars[4].shape[0] // 2
    wide = width // blocks
    span = behind[0].shape[2]
    pieces = len(behind)
    top, count = (0, rows) if part is None else (part[0] * (rows // part[1]), rows // part[1])
    done = kind in ("final", "send")
    out_shape = [jax.ShapeDtypeStruct((2, count, width), BF16 if done else F32)]
    out_shape += [jax.ShapeDtypeStruct((2, rows, units * wide), BF16) for units in sends]
    if kind == "final":
        out_shape += term_shapes(rows, width)[: 4 if part[1] == 2 else None]
    scratch = [pltpu.VMEM((2, rows, width), BF16), pltpu.SemaphoreType.DMA] if first else []
    body = functools.partial(
        fold_body, pieces=pieces, tick=tick, first=first, kind=kind, base=base, index=index, top=top, count=count, blocks=blocks
    )
    return pl.pallas_call(
        body,
        grid_spec=pltpu.PrefetchScalarGridSpec(
            num_scalar_prefetch=len(scalars),
            grid=(1,),
            in_specs=[VMEM] * (1 + 2 * pieces) + [HBM if first else VMEM],
            out_specs=[VMEM] * len(out_shape),
            scratch_shapes=scratch + [pltpu.VMEM((width, 2 * span), BF16)] * 3,
        ),
        out_shape=out_shape,
        input_output_aliases={} if first or done else {len(scalars) + 1 + 2 * pieces: 0},
        compiler_params=LIMIT,
    )(*scalars, own, *factor, *behind, before)


def term_body(pidx, pw, here, *refs, tick, count):
    rows = refs[0].shape[1]
    tile = min(rows, 256)
    for row in range(0, rows, tile):
        real = jnp.concatenate([ref[0, row : row + tile] for ref in refs[:count]], axis=1)
        imag = jnp.concatenate([ref[1, row : row + tile] for ref in refs[:count]], axis=1)
        write_term(real, imag, pidx, pw, here, tick, refs[count:], row)


def weigh(scalars, state, tick):
    out_shape = term_shapes(state[0].shape[1], sum(piece.shape[2] for piece in state))
    return pl.pallas_call(
        functools.partial(term_body, tick=tick, count=len(state)),
        grid_spec=pltpu.PrefetchScalarGridSpec(
            num_scalar_prefetch=3,
            grid=(1,),
            in_specs=[VMEM] * len(state),
            out_specs=[VMEM] * len(out_shape),
        ),
        out_shape=out_shape,
        compiler_params=LIMIT,
    )(*scalars[1:], *state)


def emit_body(*refs):
    out, sems = refs[-2:]
    parts = refs[:-2]
    high = parts[0].shape[1]
    copies = [
        pltpu.make_async_copy(ref, out.at[0, :, pl.ds(k * high, high), :], sems.at[k]) for k, ref in enumerate(parts)
    ]
    for copy in copies:
        copy.start()
    for copy in copies:
        copy.wait()


def emit(parts):
    high, width = parts[0].shape[1:]
    return pl.pallas_call(
        emit_body,
        in_specs=[VMEM] * len(parts),
        out_specs=HBM,
        out_shape=jax.ShapeDtypeStruct((1, 2, high * len(parts), width), BF16),
        scratch_shapes=[pltpu.SemaphoreType.DMA((len(parts),))],
        compiler_params=LIMIT,
        name="emit",
    )(*parts)


def picked(ref, which):
    quarter = ref.shape[1] // 2
    return jnp.where(which == 0, ref[:, :quarter], ref[:, quarter:]).astype(F32)


def pass_on_body(here, real_keep, real_got, imag_keep, imag_got, real_send, imag_send):
    major, minor = here[0] // 2, here[0] % 2
    real_send[...] = (picked(real_keep, 1 - minor) + picked(real_got, 1 - minor)).astype(BF16)
    imag_send[...] = (picked(imag_keep, 1 - major) + picked(imag_got, 1 - major)).astype(BF16)


def retain_body(here, *refs, parts, extra):
    major, minor = here[0] // 2, here[0] % 2
    out = refs[-1]
    high = refs[0].shape[0]
    for k in range(parts):
        real_keep, real_got, imag_keep, imag_got = refs[4 * k : 4 * k + 4]
        at = slice(k * high, (k + 1) * high)
        real = picked(real_keep, minor) + picked(real_got, minor)
        imag = picked(imag_keep, major) + picked(imag_got, major)
        if extra:
            real = refs[4 * parts][0, at] + real
            imag = refs[4 * parts][1, at] + imag
        out[0, at] = real
        out[1, at] = imag


def close_body(base, *refs):
    out = refs[-1]
    parts = len(refs) // 2
    high = refs[0].shape[0]
    for k in range(parts):
        at = slice(k * high, (k + 1) * high)
        out[0, at] = base[0, at] + refs[2 * k][...].astype(F32)
        out[1, at] = base[1, at] + refs[2 * k + 1][...].astype(F32)


def kernel_call(fn, scalars, args, out_shape):
    many = isinstance(out_shape, list)
    return pl.pallas_call(
        fn,
        grid_spec=pltpu.PrefetchScalarGridSpec(
            num_scalar_prefetch=len(scalars),
            grid=(1,),
            in_specs=[VMEM] * len(args),
            out_specs=[VMEM] * len(out_shape) if many else VMEM,
        ),
        out_shape=out_shape,
        compiler_params=LIMIT,
    )(*scalars, *args)


def scatter_sum(terms, before, here):
    if len(terms) == 1:
        share = lax.psum_scatter(terms[0], "pole", scatter_dimension=2, tiled=True).astype(F32)
        return share if before is None else before + share
    parts = len(terms) // 4
    high, half = terms[0].shape
    quarter = half // 2
    fields = []
    for k in range(parts):
        real_out, real_keep, imag_out, imag_keep = terms[4 * k : 4 * k + 4]
        real_got = flip(real_out, "pole", 2)
        imag_got = flip(imag_out, "pole", 1)
        fields.append((real_keep, real_got, imag_keep, imag_got))
    lasts = []
    for k in range(parts):
        sends = kernel_call(pass_on_body, (here,), fields[k], [jax.ShapeDtypeStruct((high, quarter), BF16)] * 2)
        lasts.append(flip(sends[0], "pole", 1))
        lasts.append(flip(sends[1], "pole", 2))
    extra = [] if before is None else [before]
    shape = jax.ShapeDtypeStruct((2, parts * high, quarter), F32)
    flat = [value for field in fields for value in field]
    retain = functools.partial(retain_body, parts=parts, extra=len(extra))
    base = kernel_call(retain, (here,), flat + extra, shape)
    return kernel_call(close_body, (), [base, *lasts], shape)


ARRIVE = (2, 2, 2, 1, 1)
LEAVE = (1, 2, 2, 2, 1)


def body(local_green, coupling, block_mask, state_in, pole_weight, pole_index):
    local_green, coupling, state_in = (
        pltpu.with_memory_space_constraint(value, pltpu.HBM) for value in (local_green, coupling, state_in)
    )
    ticks = coupling.shape[0]
    blocks = block_mask.shape[3]
    here = jnp.reshape(lax.axis_index("pole").astype(jnp.int32), (1,))
    mine = jnp.reshape(lax.axis_index("row").astype(jnp.int32), (1,))
    masks = row_pieces(block_mask, 2)
    state = [cut_piece(mine, here, mine, state_in, 0, ARRIVE[0], blocks)]
    plan = make_plan(mine, masks, 0)
    plan_up = shift(plan, "slab", 1)
    plan_down = shift(plan, "slab", -1)
    at = ARRIVE[0]
    for units in ARRIVE[1:]:
        state.append(cut_piece(mine, here, plan_up, state_in, at, units, blocks))
        at += units
    owns = []
    factors = []
    for tick in range(ticks):
        own = masked_factor(block_mask, coupling, tick)
        owns.append(own)
        factors.append(row_pieces(own))
    weights = (mine, jnp.transpose(pole_index, (1, 2, 0)), pole_weight, here)
    density = None
    incoming = []
    for piece in state:
        incoming.append(shift(piece, "slab", -1))
    for tick in range(ticks):
        own, factor = owns[tick], factors[tick]
        scalars = (*weights, plan_down if tick else plan)
        base = blocks if tick else 0
        before = local_green
        last_tick = tick == ticks - 1
        leaving = []
        for c, piece in enumerate(incoming):
            behind = row_pieces(piece)
            last = c == len(incoming) - 1
            kind, sends, index = "sum", (), 0
            if not last_tick and len(incoming) - c <= 3:
                kind = "send" if last else "sum"
                index = sum(LEAVE[: len(leaving)])
                sends = LEAVE[len(leaving) :] if last else LEAVE[len(leaving) : len(leaving) + 1]
            if last_tick and last:
                break
            outs = fold(scalars, own, factor, behind, before, tick, c == 0, kind, base, sends, index)
            before = outs[0]
            base += piece.shape[2] * blocks // own.shape[2]
            for block in outs[1:]:
                leaving.append(shift(block, "slab", -1))
        if last_tick:
            shapes = len(term_shapes(*own.shape[1:]))
            parts = 2 if shapes == 8 else 1
            finals = []
            terms = []
            for k in range(parts):
                outs = fold(scalars, own, factor, behind, before, tick, False, "final", base, part=(k, parts))
                finals.append(outs[0])
                terms += outs[1:]
            density = scatter_sum(terms, density, here)
            state_out = emit(finals)
        else:
            terms = weigh(scalars[:4], [before], tick)
            density = scatter_sum(terms, density, here)
        incoming = leaving
    return (state_out, density)


def solution(mesh):
    placed = (
        P(None, "pole", None, ("slab", "row"), None),
        P(None, "pole", None, ("slab", "row"), None),
        P(None, "pole", ("slab", "row"), None),
        P("pole", None, ("slab", "row"), None),
        P(),
        P(None, "pole", "slab"),
    )
    return jax.shard_map(
        body,
        mesh=mesh,
        in_specs=placed,
        out_specs=(P("pole", None, ("slab", "row"), None), P(None, ("slab", "row"), "pole")),
        check_vma=False,
    )
```

```python
import functools

import jax
import jax.numpy as jnp
from jax import lax
from jax.experimental import pallas as pl
from jax.experimental.pallas import tpu as pltpu
from jax.sharding import PartitionSpec as P


BF16 = jnp.bfloat16
F32 = jnp.float32

LIMIT = pltpu.CompilerParams(vmem_limit_bytes=20 << 20)


def shift(block, axis, step):
    devices = range(lax.axis_size(axis))
    return lax.ppermute(block, axis, [(i, i + step) for i in devices if i + step in devices])


def flip(block, axis, bit):
    return lax.ppermute(block, axis, [(i, i ^ bit) for i in range(lax.axis_size(axis))])


def row_pieces(block, dim=1):
    count = lax.axis_size("row")
    if count == 1:
        return [block]
    if count == 2:
        there = flip(block, "row", 1)
        return [block, there]
    return [lax.all_gather(block, "row", axis=dim, tiled=True)]


VMEM = pl.BlockSpec(memory_space=pltpu.VMEM)
HBM = pl.BlockSpec(memory_space=pltpu.HBM)


def mask_body(mask_ref, coupling_ref, out_ref, sems, *, tick):
    block_rows, blocks = mask_ref.shape[2:]
    rows, width = out_ref.shape[1:]
    high, wide = rows // block_rows, width // blocks

    def fetch(k):
        at = pl.ds(k * high, high)
        return pltpu.make_async_copy(coupling_ref.at[tick, 0, :, at, :], out_ref.at[:, at, :], sems.at[k])

    for k in range(block_rows):
        fetch(k).start()
    for k in range(block_rows):
        fetch(k).wait()
        rows_at = slice(k * high, (k + 1) * high)
        for col in range(blocks):
            cols = slice(col * wide, (col + 1) * wide)
            block = out_ref[:, rows_at, cols]
            keep = mask_ref[tick, 0, k, col] != 0
            out_ref[:, rows_at, cols] = jnp.where(keep, block, jnp.zeros_like(block))


def masked_factor(block_mask, coupling, tick):
    rows, width = coupling.shape[3:]
    return pl.pallas_call(
        functools.partial(mask_body, tick=tick),
        grid_spec=pltpu.PrefetchScalarGridSpec(
            num_scalar_prefetch=1,
            grid=(1,),
            in_specs=[HBM],
            out_specs=VMEM,
            scratch_shapes=[pltpu.SemaphoreType.DMA((block_mask.shape[2],))],
        ),
        out_shape=jax.ShapeDtypeStruct((2, rows, width), BF16),
        compiler_params=LIMIT,
    )(block_mask, coupling)


def dot(a, b):
    return jnp.dot(a, b, preferred_element_type=F32)


def dot_t(a, b):
    return lax.dot_general(a, b, (((1,), (1,)), ((), ())), preferred_element_type=F32)


def plan_body(mine, *refs, tick):
    out = refs[-1]
    masks = refs[:-1]
    blocks = masks[0].shape[3]
    one, none = jnp.int32(1), jnp.int32(0)
    rows = []
    for j in range(blocks):
        bits = none
        for c in range(blocks):
            if len(masks) == 1:
                value = masks[0][tick, 0, j, c]
            else:
                half = blocks // 2
                a = masks[0][tick, 0, j % half, c]
                b = masks[1][tick, 0, j % half, c]
                value = jnp.where(mine[0] == j // half, a, b)
            bits = bits + jnp.where(value != 0, jnp.int32(1 << c), none)
        rows.append(bits)

    def widest(start):
        best, found = jnp.int32(-1), none
        for c in range(2, blocks):
            both = start | (1 << c)
            count = none
            for bits in rows:
                count = count + jnp.where((bits & both) == 0, one, none)
            count = jnp.where((start & (1 << c)) != 0, jnp.int32(-1), count)
            found = jnp.where(count > best, jnp.int32(1 << c), found)
            best = jnp.maximum(best, count)
        return found

    last = widest(none)
    near = widest(last)
    soon = none
    for c in range(blocks):
        is_last = (last & (1 << c)) != 0
        is_near = (near & (1 << c)) != 0
        at = jnp.where(is_last, jnp.int32(blocks - 1), jnp.where(is_near, jnp.int32(blocks - 2), soon))
        out[at] = jnp.int32(c)
        soon = soon + jnp.where(jnp.logical_or(is_last, is_near), none, one)
    lead, next_two, rest = none, one, jnp.int32(3)
    for j in range(blocks):
        leads = jnp.logical_and((rows[j] & (last | near)) == 0, lead == 0)
        follows = jnp.logical_and((rows[j] & last) == 0, next_two < 3)
        follows = jnp.logical_and(follows, jnp.logical_not(leads))
        at = jnp.where(leads, none, jnp.where(follows, next_two, jnp.minimum(rest, blocks - 1)))
        out[blocks + at] = jnp.int32(j)
        lead = lead + jnp.where(leads, one, none)
        next_two = next_two + jnp.where(follows, one, none)
        rest = rest + jnp.where(jnp.logical_or(leads, follows), none, one)


def make_plan(mine, masks, tick):
    blocks = masks[0].shape[3]
    smem = pl.BlockSpec(memory_space=pltpu.SMEM)
    return pl.pallas_call(
        functools.partial(plan_body, tick=tick),
        grid_spec=pltpu.PrefetchScalarGridSpec(
            num_scalar_prefetch=1, grid=(1,), in_specs=[smem] * len(masks), out_specs=smem
        ),
        out_shape=jax.ShapeDtypeStruct((2 * blocks,), jnp.int32),
        compiler_params=LIMIT,
        name="plan",
    )(mine, *masks)


def cut_body(mine, here, plan, src, *refs, first, blocks):
    outs, sems = refs[:-1], refs[-1]
    wide = src.shape[3] // blocks if first else outs[0].shape[2]
    copies = []
    for out in outs:
        for u in range(out.shape[2] // wide):
            unit = len(copies)
            at = pl.ds(pl.multiple_of(plan[first + unit] * wide, wide) if first else 0, wide)
            to = slice(u * wide, (u + 1) * wide)
            copies.append(pltpu.make_async_copy(src.at[0, :, :, at], out.at[:, :, to], sems.at[unit]))
    for copy in copies:
        copy.start()
    for copy in copies:
        copy.wait()


def cut_pieces(mine, here, plan, state, first, sizes, blocks):
    rows, width = state.shape[2:]
    return pl.pallas_call(
        functools.partial(cut_body, first=first, blocks=blocks),
        grid_spec=pltpu.PrefetchScalarGridSpec(
            num_scalar_prefetch=3,
            grid=(1,),
            in_specs=[HBM],
            out_specs=[VMEM] * len(sizes),
            scratch_shapes=[pltpu.SemaphoreType.DMA((sum(sizes),))],
        ),
        out_shape=[jax.ShapeDtypeStruct((2, rows, units * width // blocks), BF16) for units in sizes],
        compiler_params=LIMIT,
    )(mine, here, plan, state)


def fold_body(*refs, pieces, tick, first, kind, base, index, top, count, blocks):
    mine, pidx, pw, here, plan = refs[:5]
    own = refs[5]
    refs = refs[6:]
    factor = refs[:pieces]
    behind = refs[pieces : 2 * pieces]
    before = refs[2 * pieces]
    right, low, high = refs[-3:]
    outs = refs[1 + 2 * pieces : -3]
    span = behind[0].shape[2]
    wide = own.shape[2] // blocks

    def block_cols(index):
        return pl.ds(pl.multiple_of(plan[index] * wide, wide), wide)

    if first:
        green, sem = outs[-2:]
        outs = outs[:-2]
        fetch = pltpu.make_async_copy(before.at[tick, 0], green, sem)
        fetch.start()
    for k in range(pieces):
        size = behind[k].shape[1]
        at = slice(0, size)
        if pieces == 2:
            at = pl.ds(pl.multiple_of((mine[0] if k == 0 else 1 - mine[0]) * size, size), size)
        right[at, :span] = behind[k][0]
        right[at, span:] = behind[k][1]
        for u in range(span // wide):
            cols = block_cols(base + u)
            real = factor[k][0, :, cols]
            imag = factor[k][1, :, cols]
            one = slice(u * wide, (u + 1) * wide)
            two = slice(span + u * wide, span + (u + 1) * wide)
            low[at, one] = real
            low[at, two] = -imag
            high[at, one] = imag
            high[at, two] = real
    tile = min(count, 256)
    for step in range(count // tile):
        at = slice(top + step * tile, top + (step + 1) * tile)
        to = slice(step * tile, (step + 1) * tile)
        a = dot(own[0, at], right[...])
        b = dot(own[1, at], right[...])
        half = jnp.concatenate([a[:, :span] - b[:, span:], a[:, span:] + b[:, :span]], axis=1).astype(BF16)
        real = dot_t(half, low[...])
        imag = dot_t(half, high[...])
        if first:
            if step == 0:
                fetch.wait()
            real = green[0, at].astype(F32) + real
            imag = green[1, at].astype(F32) + imag
        else:
            real = before[0, at] + real
            imag = before[1, at] + imag
        outs[0][0, to] = real.astype(outs[0].dtype)
        outs[0][1, to] = imag.astype(outs[0].dtype)
        if kind == "final":
            write_term(real.astype(BF16), imag.astype(BF16), pidx, pw, here, tick, outs[1:], step * tile)
            continue
        at_block = blocks + index
        for out in outs[1:]:
            for u in range(out.shape[2] // wide):
                for part in range(2):
                    out[part, to, u * wide : (u + 1) * wide] = outs[0][part, to, block_cols(at_block)].astype(BF16)
                at_block += 1


def write_term(real, imag, pidx, pw, here, tick, outs, row):
    real = real.astype(F32)
    imag = imag.astype(F32)
    w0 = pw[0, pidx[0, 0, tick]]
    w1 = pw[1, pidx[0, 0, tick]]
    term_real = (w0 * real - w1 * imag).astype(BF16)
    term_imag = (w0 * imag + w1 * real).astype(BF16)
    high, width = real.shape
    if len(outs) == 1:
        outs[0][0, row : row + high] = term_real
        outs[0][1, row : row + high] = term_imag
        return
    part = row // outs[0].shape[0]
    row -= part * outs[0].shape[0]
    at = slice(row, row + high)
    real_send, real_keep, imag_send, imag_keep = outs[4 * part : 4 * part + 4]
    quarter = width // 4
    first_major = here[0] // 2 == 0
    first_minor = here[0] % 2 == 0
    lower, upper = term_real[:, : 2 * quarter], term_real[:, 2 * quarter :]
    real_send[at] = jnp.where(first_major, upper, lower)
    real_keep[at] = jnp.where(first_major, lower, upper)
    for pair in range(2):
        cols = slice(pair * quarter, (pair + 1) * quarter)
        even = term_imag[:, 2 * pair * quarter : (2 * pair + 1) * quarter]
        odd = term_imag[:, (2 * pair + 1) * quarter : (2 * pair + 2) * quarter]
        imag_send[at, cols] = jnp.where(first_minor, odd, even)
        imag_keep[at, cols] = jnp.where(first_minor, even, odd)


def term_shapes(rows, width):
    if lax.axis_size("pole") != 4:
        return [jax.ShapeDtypeStruct((2, rows, width), BF16)]
    parts = 2 if rows % 512 == 0 else 1
    return [jax.ShapeDtypeStruct((rows // parts, width // 2), BF16)] * (4 * parts)


def fold(scalars, own, factor, behind, before, tick, first, kind, base, sends=(), index=0, part=None):
    rows, width = own.shape[1:]
    blocks = scalars[4].shape[0] // 2
    wide = width // blocks
    span = behind[0].shape[2]
    pieces = len(behind)
    top, count = (0, rows) if part is None else (part[0] * (rows // part[1]), rows // part[1])
    done = kind in ("final", "send")
    out_shape = [jax.ShapeDtypeStruct((2, count, width), BF16 if done else F32)]
    out_shape += [jax.ShapeDtypeStruct((2, rows, units * wide), BF16) for units in sends]
    if kind == "final":
        out_shape += term_shapes(rows, width)[: 4 if part[1] == 2 else None]
    scratch = [pltpu.VMEM((2, rows, width), BF16), pltpu.SemaphoreType.DMA] if first else []
    body = functools.partial(
        fold_body, pieces=pieces, tick=tick, first=first, kind=kind, base=base, index=index, top=top, count=count, blocks=blocks
    )
    return pl.pallas_call(
        body,
        grid_spec=pltpu.PrefetchScalarGridSpec(
            num_scalar_prefetch=len(scalars),
            grid=(1,),
            in_specs=[VMEM] * (1 + 2 * pieces) + [HBM if first else VMEM],
            out_specs=[VMEM] * len(out_shape),
            scratch_shapes=scratch + [pltpu.VMEM((width, 2 * span), BF16)] * 3,
        ),
        out_shape=out_shape,
        input_output_aliases={} if first or done else {len(scalars) + 1 + 2 * pieces: 0},
        compiler_params=LIMIT,
    )(*scalars, own, *factor, *behind, before)


def term_body(pidx, pw, here, *refs, tick, count):
    rows = refs[0].shape[1]
    tile = min(rows, 256)
    for row in range(0, rows, tile):
        real = jnp.concatenate([ref[0, row : row + tile] for ref in refs[:count]], axis=1)
        imag = jnp.concatenate([ref[1, row : row + tile] for ref in refs[:count]], axis=1)
        write_term(real, imag, pidx, pw, here, tick, refs[count:], row)


def weigh(scalars, state, tick):
    out_shape = term_shapes(state[0].shape[1], sum(piece.shape[2] for piece in state))
    return pl.pallas_call(
        functools.partial(term_body, tick=tick, count=len(state)),
        grid_spec=pltpu.PrefetchScalarGridSpec(
            num_scalar_prefetch=3,
            grid=(1,),
            in_specs=[VMEM] * len(state),
            out_specs=[VMEM] * len(out_shape),
        ),
        out_shape=out_shape,
        compiler_params=LIMIT,
    )(*scalars[1:], *state)


def emit_body(*refs):
    out, sems = refs[-2:]
    parts = refs[:-2]
    high = parts[0].shape[1]
    copies = [
        pltpu.make_async_copy(ref, out.at[0, :, pl.ds(k * high, high), :], sems.at[k]) for k, ref in enumerate(parts)
    ]
    for copy in copies:
        copy.start()
    for copy in copies:
        copy.wait()


def emit(parts):
    high, width = parts[0].shape[1:]
    return pl.pallas_call(
        emit_body,
        in_specs=[VMEM] * len(parts),
        out_specs=HBM,
        out_shape=jax.ShapeDtypeStruct((1, 2, high * len(parts), width), BF16),
        scratch_shapes=[pltpu.SemaphoreType.DMA((len(parts),))],
        compiler_params=LIMIT,
        name="emit",
    )(*parts)


def picked(ref, which):
    quarter = ref.shape[1] // 2
    return jnp.where(which == 0, ref[:, :quarter], ref[:, quarter:]).astype(F32)


def pass_on_body(here, real_keep, real_got, imag_keep, imag_got, real_send, imag_send):
    major, minor = here[0] // 2, here[0] % 2
    real_send[...] = (picked(real_keep, 1 - minor) + picked(real_got, 1 - minor)).astype(BF16)
    imag_send[...] = (picked(imag_keep, 1 - major) + picked(imag_got, 1 - major)).astype(BF16)


def retain_body(here, *refs, parts, extra):
    major, minor = here[0] // 2, here[0] % 2
    out = refs[-1]
    high = refs[0].shape[0]
    for k in range(parts):
        real_keep, real_got, imag_keep, imag_got = refs[4 * k : 4 * k + 4]
        at = slice(k * high, (k + 1) * high)
        real = picked(real_keep, minor) + picked(real_got, minor)
        imag = picked(imag_keep, major) + picked(imag_got, major)
        if extra:
            real = refs[4 * parts][0, at] + real
            imag = refs[4 * parts][1, at] + imag
        out[0, at] = real
        out[1, at] = imag


def close_body(base, *refs):
    out = refs[-1]
    parts = len(refs) // 2
    high = refs[0].shape[0]
    for k in range(parts):
        at = slice(k * high, (k + 1) * high)
        out[0, at] = base[0, at] + refs[2 * k][...].astype(F32)
        out[1, at] = base[1, at] + refs[2 * k + 1][...].astype(F32)


def kernel_call(fn, scalars, args, out_shape):
    many = isinstance(out_shape, list)
    return pl.pallas_call(
        fn,
        grid_spec=pltpu.PrefetchScalarGridSpec(
            num_scalar_prefetch=len(scalars),
            grid=(1,),
            in_specs=[VMEM] * len(args),
            out_specs=[VMEM] * len(out_shape) if many else VMEM,
        ),
        out_shape=out_shape,
        compiler_params=LIMIT,
    )(*scalars, *args)


def scatter_sum(terms, before, here):
    if len(terms) == 1:
        share = lax.psum_scatter(terms[0], "pole", scatter_dimension=2, tiled=True).astype(F32)
        return share if before is None else before + share
    parts = len(terms) // 4
    high, half = terms[0].shape
    quarter = half // 2
    fields = []
    for k in range(parts):
        real_out, real_keep, imag_out, imag_keep = terms[4 * k : 4 * k + 4]
        real_got = flip(real_out, "pole", 2)
        imag_got = flip(imag_out, "pole", 1)
        fields.append((real_keep, real_got, imag_keep, imag_got))
    lasts = []
    for k in range(parts):
        sends = kernel_call(pass_on_body, (here,), fields[k], [jax.ShapeDtypeStruct((high, quarter), BF16)] * 2)
        lasts.append(flip(sends[0], "pole", 1))
        lasts.append(flip(sends[1], "pole", 2))
    extra = [] if before is None else [before]
    shape = jax.ShapeDtypeStruct((2, parts * high, quarter), F32)
    flat = [value for field in fields for value in field]
    retain = functools.partial(retain_body, parts=parts, extra=len(extra))
    base = kernel_call(retain, (here,), flat + extra, shape)
    return kernel_call(close_body, (), [base, *lasts], shape)


ARRIVE = (2, 2, 2, 1, 1)
LEAVE = (1, 2, 2, 2, 1)


def body(local_green, coupling, block_mask, state_in, pole_weight, pole_index):
    local_green, coupling, state_in = (
        pltpu.with_memory_space_constraint(value, pltpu.HBM) for value in (local_green, coupling, state_in)
    )
    ticks = coupling.shape[0]
    blocks = block_mask.shape[3]
    here = jnp.reshape(lax.axis_index("pole").astype(jnp.int32), (1,))
    mine = jnp.reshape(lax.axis_index("row").astype(jnp.int32), (1,))
    masks = row_pieces(block_mask, 2)
    state = cut_pieces(mine, here, mine, state_in, 0, ARRIVE[:1], blocks)
    plan = make_plan(mine, masks, 0)
    plan_up = shift(plan, "slab", 1)
    plan_down = shift(plan, "slab", -1)
    state += cut_pieces(mine, here, plan_up, state_in, ARRIVE[0], ARRIVE[1:2], blocks)
    state += cut_pieces(mine, here, plan_up, state_in, sum(ARRIVE[:2]), ARRIVE[2:], blocks)
    owns = []
    factors = []
    for tick in range(ticks):
        own = masked_factor(block_mask, coupling, tick)
        owns.append(own)
        factors.append(row_pieces(own))
    weights = (mine, jnp.transpose(pole_index, (1, 2, 0)), pole_weight, here)
    density = None
    incoming = []
    for piece in state:
        incoming.append(shift(piece, "slab", -1))
    for tick in range(ticks):
        own, factor = owns[tick], factors[tick]
        scalars = (*weights, plan_down if tick else plan)
        base = blocks if tick else 0
        before = local_green
        last_tick = tick == ticks - 1
        leaving = []
        for c, piece in enumerate(incoming):
            behind = row_pieces(piece)
            last = c == len(incoming) - 1
            kind, sends, index = "sum", (), 0
            if not last_tick and len(incoming) - c <= 3:
                kind = "send" if last else "sum"
                index = sum(LEAVE[: len(leaving)])
                sends = LEAVE[len(leaving) :] if last else LEAVE[len(leaving) : len(leaving) + 1]
            if last_tick and last:
                break
            outs = fold(scalars, own, factor, behind, before, tick, c == 0, kind, base, sends, index)
            before = outs[0]
            base += piece.shape[2] * blocks // own.shape[2]
            for block in outs[1:]:
                leaving.append(shift(block, "slab", -1))
        if last_tick:
            shapes = len(term_shapes(*own.shape[1:]))
            parts = 2 if shapes == 8 else 1
            finals = []
            terms = []
            for k in range(parts):
                outs = fold(scalars, own, factor, behind, before, tick, False, "final", base, part=(k, parts))
                finals.append(outs[0])
                terms += outs[1:]
            density = scatter_sum(terms, density, here)
            state_out = emit(finals)
        else:
            terms = weigh(scalars[:4], [before], tick)
            density = scatter_sum(terms, density, here)
        incoming = leaving
    return (state_out, density)


def solution(mesh):
    placed = (
        P(None, "pole", None, ("slab", "row"), None),
        P(None, "pole", None, ("slab", "row"), None),
        P(None, "pole", ("slab", "row"), None),
        P("pole", None, ("slab", "row"), None),
        P(),
        P(None, "pole", "slab"),
    )
    return jax.shard_map(
        body,
        mesh=mesh,
        in_specs=placed,
        out_specs=(P("pole", None, ("slab", "row"), None), P(None, ("slab", "row"), "pole")),
        check_vma=False,
    )
```

```python
import functools

import jax
import jax.numpy as jnp
from jax import lax
from jax.experimental import pallas as pl
from jax.experimental.pallas import tpu as pltpu
from jax.sharding import PartitionSpec as P


BF16 = jnp.bfloat16
F32 = jnp.float32

LIMIT = pltpu.CompilerParams(vmem_limit_bytes=20 << 20)


def shift(block, axis, step):
    devices = range(lax.axis_size(axis))
    return lax.ppermute(block, axis, [(i, i + step) for i in devices if i + step in devices])


def flip(block, axis, bit):
    return lax.ppermute(block, axis, [(i, i ^ bit) for i in range(lax.axis_size(axis))])


def row_pieces(block, dim=1):
    count = lax.axis_size("row")
    if count == 1:
        return [block]
    if count == 2:
        there = flip(block, "row", 1)
        return [block, there]
    return [lax.all_gather(block, "row", axis=dim, tiled=True)]


VMEM = pl.BlockSpec(memory_space=pltpu.VMEM)
HBM = pl.BlockSpec(memory_space=pltpu.HBM)


def mask_body(mask_ref, coupling_ref, out_ref, sems, *, tick):
    block_rows, blocks = mask_ref.shape[2:]
    rows, width = out_ref.shape[1:]
    high, wide = rows // block_rows, width // blocks

    def fetch(k):
        at = pl.ds(k * high, high)
        return pltpu.make_async_copy(coupling_ref.at[tick, 0, :, at, :], out_ref.at[:, at, :], sems.at[k])

    for k in range(block_rows):
        fetch(k).start()
    for k in range(block_rows):
        fetch(k).wait()
        rows_at = slice(k * high, (k + 1) * high)
        for col in range(blocks):
            cols = slice(col * wide, (col + 1) * wide)
            block = out_ref[:, rows_at, cols]
            keep = mask_ref[tick, 0, k, col] != 0
            out_ref[:, rows_at, cols] = jnp.where(keep, block, jnp.zeros_like(block))


def masked_factor(block_mask, coupling, tick):
    rows, width = coupling.shape[3:]
    return pl.pallas_call(
        functools.partial(mask_body, tick=tick),
        grid_spec=pltpu.PrefetchScalarGridSpec(
            num_scalar_prefetch=1,
            grid=(1,),
            in_specs=[HBM],
            out_specs=VMEM,
            scratch_shapes=[pltpu.SemaphoreType.DMA((block_mask.shape[2],))],
        ),
        out_shape=jax.ShapeDtypeStruct((2, rows, width), BF16),
        compiler_params=LIMIT,
    )(block_mask, coupling)


def dot(a, b):
    return jnp.dot(a, b, preferred_element_type=F32)


def dot_t(a, b):
    return lax.dot_general(a, b, (((1,), (1,)), ((), ())), preferred_element_type=F32)


def plan_body(mine, *refs, tick):
    out = refs[-1]
    masks = refs[:-1]
    blocks = masks[0].shape[3]
    one, none = jnp.int32(1), jnp.int32(0)
    rows = []
    for j in range(blocks):
        bits = none
        for c in range(blocks):
            if len(masks) == 1:
                value = masks[0][tick, 0, j, c]
            else:
                half = blocks // 2
                a = masks[0][tick, 0, j % half, c]
                b = masks[1][tick, 0, j % half, c]
                value = jnp.where(mine[0] == j // half, a, b)
            bits = bits + jnp.where(value != 0, jnp.int32(1 << c), none)
        rows.append(bits)

    def widest(start):
        best, found = jnp.int32(-1), none
        for c in range(2, blocks):
            both = start | (1 << c)
            count = none
            for bits in rows:
                count = count + jnp.where((bits & both) == 0, one, none)
            count = jnp.where((start & (1 << c)) != 0, jnp.int32(-1), count)
            found = jnp.where(count > best, jnp.int32(1 << c), found)
            best = jnp.maximum(best, count)
        return found

    last = widest(none)
    near = widest(last)
    soon = none
    for c in range(blocks):
        is_last = (last & (1 << c)) != 0
        is_near = (near & (1 << c)) != 0
        at = jnp.where(is_last, jnp.int32(blocks - 1), jnp.where(is_near, jnp.int32(blocks - 2), soon))
        out[at] = jnp.int32(c)
        soon = soon + jnp.where(jnp.logical_or(is_last, is_near), none, one)
    lead, next_two, rest = none, one, jnp.int32(3)
    for j in range(blocks):
        leads = jnp.logical_and((rows[j] & (last | near)) == 0, lead == 0)
        follows = jnp.logical_and((rows[j] & last) == 0, next_two < 3)
        follows = jnp.logical_and(follows, jnp.logical_not(leads))
        at = jnp.where(leads, none, jnp.where(follows, next_two, jnp.minimum(rest, blocks - 1)))
        out[blocks + at] = jnp.int32(j)
        lead = lead + jnp.where(leads, one, none)
        next_two = next_two + jnp.where(follows, one, none)
        rest = rest + jnp.where(jnp.logical_or(leads, follows), none, one)


def make_plan(mine, masks, tick):
    blocks = masks[0].shape[3]
    smem = pl.BlockSpec(memory_space=pltpu.SMEM)
    return pl.pallas_call(
        functools.partial(plan_body, tick=tick),
        grid_spec=pltpu.PrefetchScalarGridSpec(
            num_scalar_prefetch=1, grid=(1,), in_specs=[smem] * len(masks), out_specs=smem
        ),
        out_shape=jax.ShapeDtypeStruct((2 * blocks,), jnp.int32),
        compiler_params=LIMIT,
        name="plan",
    )(mine, *masks)


def cut_body(mine, here, plan, src, *refs, first, blocks):
    outs, sems = refs[:-1], refs[-1]
    wide = src.shape[3] // blocks if first else outs[0].shape[2]
    copies = []
    for out in outs:
        for u in range(out.shape[2] // wide):
            unit = len(copies)
            at = pl.ds(pl.multiple_of(plan[first + unit] * wide, wide) if first else 0, wide)
            to = slice(u * wide, (u + 1) * wide)
            copies.append(pltpu.make_async_copy(src.at[0, :, :, at], out.at[:, :, to], sems.at[unit]))
    for copy in copies:
        copy.start()
    for copy in copies:
        copy.wait()


def cut_pieces(mine, here, plan, state, first, sizes, blocks):
    rows, width = state.shape[2:]
    return pl.pallas_call(
        functools.partial(cut_body, first=first, blocks=blocks),
        grid_spec=pltpu.PrefetchScalarGridSpec(
            num_scalar_prefetch=3,
            grid=(1,),
            in_specs=[HBM],
            out_specs=[VMEM] * len(sizes),
            scratch_shapes=[pltpu.SemaphoreType.DMA((sum(sizes),))],
        ),
        out_shape=[jax.ShapeDtypeStruct((2, rows, units * width // blocks), BF16) for units in sizes],
        compiler_params=LIMIT,
    )(mine, here, plan, state)


def fold_body(*refs, pieces, tick, first, kind, base, index, top, count, blocks):
    mine, pidx, pw, here, plan = refs[:5]
    own = refs[5]
    refs = refs[6:]
    factor = refs[:pieces]
    behind = refs[pieces : 2 * pieces]
    before = refs[2 * pieces]
    outs = refs[1 + 2 * pieces :]
    span = behind[0].shape[2]
    wide = own.shape[2] // blocks

    def block_cols(at_block):
        return pl.ds(pl.multiple_of(plan[at_block] * wide, wide), wide)

    def offset(k):
        size = behind[k].shape[1]
        return 0 if pieces == 1 else pl.multiple_of((mine[0] if k == 0 else 1 - mine[0]) * size, size)

    if first:
        green, sem = outs[-2:]
        outs = outs[:-2]
        fetch = pltpu.make_async_copy(before.at[tick, 0], green, sem)
        fetch.start()
    if kind == "final":
        term = outs[-1]
        outs = outs[:-1]
    units = [block_cols(base + u) for u in range(span // wide)]
    tile = min(count, 256)
    for step in range(count // tile):
        at = slice(top + step * tile, top + (step + 1) * tile)
        to = slice(step * tile, (step + 1) * tile)
        both = None
        for k in range(pieces):
            inner = pl.ds(offset(k), behind[k].shape[1])
            left = jnp.concatenate([own[0, at, inner], own[1, at, inner]], axis=0)
            share = dot(left, jnp.concatenate([behind[k][0], behind[k][1]], axis=1))
            both = share if both is None else both + share
        real = both[:tile, :span] - both[tile:, span:]
        imag = both[:tile, span:] + both[tile:, :span]
        left = jnp.concatenate(
            [jnp.concatenate([real, -imag], axis=1), jnp.concatenate([imag, real], axis=1)], axis=0
        ).astype(BF16)
        if first and step == 0:
            fetch.wait()
        for k in range(pieces):
            size = behind[k].shape[1]
            group = min(size, 256)
            for start in range(0, size, group):
                rows = slice(start, start + group)
                right = jnp.concatenate([factor[k][part, rows, cols] for part in range(2) for cols in units], axis=1)
                pair = dot_t(left, right)
                cols = pl.ds(offset(k) + start, group)
                if pieces == 2:
                    cols = pl.ds(pl.multiple_of(offset(k) + start, group), group)
                values = []
                for part in range(2):
                    value = pair[part * tile : (part + 1) * tile]
                    if first:
                        value = green[part, at, cols].astype(F32) + value
                    else:
                        value = before[part, at, cols] + value
                    value = value.astype(outs[0].dtype)
                    outs[0][part, to, cols] = value
                    values.append(value)
                if kind == "final":
                    weighted = weigh_pair(values, pidx, pw, tick)
                    term[0, to, cols] = weighted[0]
                    term[1, to, cols] = weighted[1]
        if kind == "final":
            deal_term(term, here, outs[1:], to)
            continue
        at_block = blocks + index
        for out in outs[1:]:
            for u in range(out.shape[2] // wide):
                for part in range(2):
                    out[part, to, u * wide : (u + 1) * wide] = outs[0][part, to, block_cols(at_block)].astype(BF16)
                at_block += 1


def weigh_pair(values, pidx, pw, tick):
    real, imag = (value.astype(F32) for value in values)
    w0 = pw[0, pidx[0, 0, tick]]
    w1 = pw[1, pidx[0, 0, tick]]
    return (w0 * real - w1 * imag).astype(BF16), (w0 * imag + w1 * real).astype(BF16)


def deal_term(term, here, outs, at):
    if len(outs) == 1:
        outs[0][:, at] = term[:, at]
        return
    real_send, real_keep, imag_send, imag_keep = outs
    quarter = term.shape[2] // 4
    major, minor = here[0] // 2, here[0] % 2

    def cut(part, start, size):
        return term[part, at, pl.ds(pl.multiple_of(start * quarter, quarter), size * quarter)]

    real_send[at] = cut(0, 2 * (1 - major), 2)
    real_keep[at] = cut(0, 2 * major, 2)
    for pair in range(2):
        cols = slice(pair * quarter, (pair + 1) * quarter)
        imag_send[at, cols] = cut(1, 2 * pair + 1 - minor, 1)
        imag_keep[at, cols] = cut(1, 2 * pair + minor, 1)


def term_shapes(rows, width):
    if lax.axis_size("pole") != 4:
        return [jax.ShapeDtypeStruct((2, rows, width), BF16)]
    return [jax.ShapeDtypeStruct((rows, width // 2), BF16)] * 4


def row_parts(rows):
    if rows % 512 or lax.axis_size("pole") != 4:
        return [(0, rows)]
    unit = rows // 4
    return [(0, unit), (unit, 2 * unit), (3 * unit, unit)]


def fold(scalars, own, factor, behind, before, tick, first, kind, base, sends=(), index=0, part=None):
    rows, width = own.shape[1:]
    blocks = scalars[4].shape[0] // 2
    wide = width // blocks
    pieces = len(behind)
    top, count = part or (0, rows)
    done = kind in ("final", "send")
    out_shape = [jax.ShapeDtypeStruct((2, count, width), BF16 if done else F32)]
    out_shape += [jax.ShapeDtypeStruct((2, rows, units * wide), BF16) for units in sends]
    scratch = [pltpu.VMEM((2, rows, width), BF16), pltpu.SemaphoreType.DMA] if first else []
    if kind == "final":
        out_shape += term_shapes(count, width)
        scratch = [pltpu.VMEM((2, count, width), BF16)]
    body = functools.partial(
        fold_body, pieces=pieces, tick=tick, first=first, kind=kind, base=base, index=index, top=top, count=count, blocks=blocks
    )
    return pl.pallas_call(
        body,
        grid_spec=pltpu.PrefetchScalarGridSpec(
            num_scalar_prefetch=len(scalars),
            grid=(1,),
            in_specs=[VMEM] * (1 + 2 * pieces) + [HBM if first else VMEM],
            out_specs=[VMEM] * len(out_shape),
            scratch_shapes=scratch,
        ),
        out_shape=out_shape,
        input_output_aliases={} if first or done else {len(scalars) + 1 + 2 * pieces: 0},
        compiler_params=LIMIT,
    )(*scalars, own, *factor, *behind, before)


def term_body(pidx, pw, here, state, *refs, tick):
    outs, term = refs[:-1], refs[-1]
    rows, width = state.shape[1:]
    tile = min(rows, 128)
    group = min(width, 256)
    for row in range(0, rows, tile):
        at = slice(row, row + tile)
        for col in range(0, width, group):
            cols = slice(col, col + group)
            weighted = weigh_pair([state[part, at, cols] for part in range(2)], pidx, pw, tick)
            term[0, at, cols] = weighted[0]
            term[1, at, cols] = weighted[1]
        deal_term(term, here, outs, at)


def weigh(scalars, state, tick):
    out_shape = term_shapes(*state.shape[1:])
    return pl.pallas_call(
        functools.partial(term_body, tick=tick),
        grid_spec=pltpu.PrefetchScalarGridSpec(
            num_scalar_prefetch=3,
            grid=(1,),
            in_specs=[VMEM],
            out_specs=[VMEM] * len(out_shape),
            scratch_shapes=[pltpu.VMEM(state.shape, BF16)],
        ),
        out_shape=out_shape,
        compiler_params=LIMIT,
    )(*scalars[1:], state)


def emit_body(*refs):
    out, sems = refs[-2:]
    copies = []
    row = 0
    for k, ref in enumerate(refs[:-2]):
        high = ref.shape[1]
        copies.append(pltpu.make_async_copy(ref, out.at[0, :, pl.ds(row, high), :], sems.at[k]))
        row += high
    for copy in copies:
        copy.start()
    for copy in copies:
        copy.wait()


def emit(parts):
    rows, width = sum(part.shape[1] for part in parts), parts[0].shape[2]
    return pl.pallas_call(
        emit_body,
        in_specs=[VMEM] * len(parts),
        out_specs=HBM,
        out_shape=jax.ShapeDtypeStruct((1, 2, rows, width), BF16),
        scratch_shapes=[pltpu.SemaphoreType.DMA((len(parts),))],
        compiler_params=LIMIT,
        name="emit",
    )(*parts)


def picked(ref, which):
    quarter = ref.shape[1] // 2
    return jnp.where(which == 0, ref[:, :quarter], ref[:, quarter:]).astype(F32)


def pass_on_body(here, real_keep, real_got, imag_keep, imag_got, real_send, imag_send):
    major, minor = here[0] // 2, here[0] % 2
    real_send[...] = (picked(real_keep, 1 - minor) + picked(real_got, 1 - minor)).astype(BF16)
    imag_send[...] = (picked(imag_keep, 1 - major) + picked(imag_got, 1 - major)).astype(BF16)


def retain_body(here, *refs, parts, extra):
    major, minor = here[0] // 2, here[0] % 2
    out = refs[-1]
    row = 0
    for k in range(parts):
        real_keep, real_got, imag_keep, imag_got = refs[4 * k : 4 * k + 4]
        at = slice(row, row + real_keep.shape[0])
        row = at.stop
        real = picked(real_keep, minor) + picked(real_got, minor)
        imag = picked(imag_keep, major) + picked(imag_got, major)
        if extra:
            real = refs[4 * parts][0, at] + real
            imag = refs[4 * parts][1, at] + imag
        out[0, at] = real
        out[1, at] = imag


def close_body(base, *refs, top, write):
    if write:
        out, total, sem = refs[-3:]
        lasts = refs[:-4] if top else refs[:-3]
        row = top
    else:
        total = refs[-1]
        lasts = refs[:-1]
        row = 0
    first = row
    for k in range(len(lasts) // 2):
        at = slice(row, row + lasts[2 * k].shape[0])
        to = slice(row - first, at.stop - first)
        row = at.stop
        total[0, to] = base[0, at] + lasts[2 * k][...].astype(F32)
        total[1, to] = base[1, at] + lasts[2 * k + 1][...].astype(F32)
    if write:
        copy = pltpu.make_async_copy(total, out.at[:, pl.ds(first, row - first), :], sem)
        copy.start()
        copy.wait()


def close_out(base, lasts, top, whole):
    high = sum(last.shape[0] for last in lasts[::2])
    args = [base, *lasts] + ([whole] if top else [])
    return pl.pallas_call(
        functools.partial(close_body, top=top, write=True),
        in_specs=[VMEM] * (1 + len(lasts)) + ([HBM] if top else []),
        out_specs=HBM,
        out_shape=jax.ShapeDtypeStruct(base.shape, F32),
        scratch_shapes=[pltpu.VMEM((2, high, base.shape[2]), F32), pltpu.SemaphoreType.DMA],
        input_output_aliases={len(args) - 1: 0} if top else {},
        compiler_params=LIMIT,
    )(*args)


def kernel_call(fn, scalars, args, out_shape):
    many = isinstance(out_shape, list)
    return pl.pallas_call(
        fn,
        grid_spec=pltpu.PrefetchScalarGridSpec(
            num_scalar_prefetch=len(scalars),
            grid=(1,),
            in_specs=[VMEM] * len(args),
            out_specs=[VMEM] * len(out_shape) if many else VMEM,
        ),
        out_shape=out_shape,
        compiler_params=LIMIT,
    )(*scalars, *args)


def scatter_sum(terms, before, here, last):
    if len(terms[0]) == 1:
        share = lax.psum_scatter(terms[0][0], "pole", scatter_dimension=2, tiled=True).astype(F32)
        return share if before is None else before + share
    fields = []
    for real_out, real_keep, imag_out, imag_keep in terms:
        real_got = flip(real_out, "pole", 2)
        imag_got = flip(imag_out, "pole", 1)
        fields.append((real_keep, real_got, imag_keep, imag_got))
    lasts = []
    for field in fields:
        high, half = field[0].shape
        send = jax.ShapeDtypeStruct((high, half // 2), BF16)
        sends = kernel_call(pass_on_body, (here,), field, [send] * 2)
        real_last = flip(sends[0], "pole", 1)
        imag_last = flip(sends[1], "pole", 2)
        lasts.append((real_last, imag_last))
    extra = [] if before is None else [before]
    rows = sum(field[0].shape[0] for field in fields)
    shape = jax.ShapeDtypeStruct((2, rows, half // 2), F32)
    flat = [value for field in fields for value in field]
    retain = functools.partial(retain_body, parts=len(fields), extra=len(extra))
    base = kernel_call(retain, (here,), flat + extra, shape)
    if not last:
        close = functools.partial(close_body, top=0, write=False)
        return kernel_call(close, (), [base, *(v for pair in lasts for v in pair)], shape)
    whole = None
    top = 0
    groups = [lasts[:-1], lasts[-1:]] if len(lasts) > 1 else [lasts]
    for group in groups:
        flat = [value for pair in group for value in pair]
        whole = close_out(base, flat, top, whole)
        top += sum(pair[0].shape[0] for pair in group)
    return whole


ARRIVE = (2, 2, 2, 1, 1)
LEAVE = (1, 2, 2, 2, 1)


def body(local_green, coupling, block_mask, state_in, pole_weight, pole_index):
    local_green, coupling, state_in = (
        pltpu.with_memory_space_constraint(value, pltpu.HBM) for value in (local_green, coupling, state_in)
    )
    ticks = coupling.shape[0]
    blocks = block_mask.shape[3]
    here = jnp.reshape(lax.axis_index("pole").astype(jnp.int32), (1,))
    mine = jnp.reshape(lax.axis_index("row").astype(jnp.int32), (1,))
    masks = row_pieces(block_mask, 2)
    state = cut_pieces(mine, here, mine, state_in, 0, ARRIVE[:1], blocks)
    plan = make_plan(mine, masks, 0)
    plan_up = shift(plan, "slab", 1)
    plan_down = shift(plan, "slab", -1)
    state += cut_pieces(mine, here, plan_up, state_in, ARRIVE[0], ARRIVE[1:2], blocks)
    state += cut_pieces(mine, here, plan_up, state_in, sum(ARRIVE[:2]), ARRIVE[2:], blocks)
    owns = []
    factors = []
    for tick in range(ticks):
        own = masked_factor(block_mask, coupling, tick)
        owns.append(own)
        factors.append(row_pieces(own))
    weights = (mine, jnp.transpose(pole_index, (1, 2, 0)), pole_weight, here)
    density = None
    incoming = []
    for piece in state:
        incoming.append(shift(piece, "slab", -1))
    for tick in range(ticks):
        own, factor = owns[tick], factors[tick]
        scalars = (*weights, plan_down if tick else plan)
        base = blocks if tick else 0
        before = local_green
        last_tick = tick == ticks - 1
        leaving = []
        for c, piece in enumerate(incoming):
            behind = row_pieces(piece)
            last = c == len(incoming) - 1
            kind, sends, index = "sum", (), 0
            if not last_tick and len(incoming) - c <= 3:
                kind = "send" if last else "sum"
                index = sum(LEAVE[: len(leaving)])
                sends = LEAVE[len(leaving) :] if last else LEAVE[len(leaving) : len(leaving) + 1]
            if last_tick and last:
                break
            outs = fold(scalars, own, factor, behind, before, tick, c == 0, kind, base, sends, index)
            before = outs[0]
            base += piece.shape[2] * blocks // own.shape[2]
            for block in outs[1:]:
                leaving.append(shift(block, "slab", -1))
        if last_tick:
            finals = []
            terms = []
            for part in row_parts(own.shape[1]):
                outs = fold(scalars, own, factor, behind, before, tick, False, "final", base, part=part)
                finals.append(outs[0])
                terms.append(outs[1:])
            density = scatter_sum(terms, density, here, True)
            state_out = emit(finals)
        else:
            terms = weigh(scalars[:4], before, tick)
            density = scatter_sum([terms], density, here, False)
        incoming = leaving
    return (state_out, density)


def solution(mesh):
    placed = (
        P(None, "pole", None, ("slab", "row"), None),
        P(None, "pole", None, ("slab", "row"), None),
        P(None, "pole", ("slab", "row"), None),
        P("pole", None, ("slab", "row"), None),
        P(),
        P(None, "pole", "slab"),
    )
    return jax.shard_map(
        body,
        mesh=mesh,
        in_specs=placed,
        out_specs=(P("pole", None, ("slab", "row"), None), P(None, ("slab", "row"), "pole")),
        check_vma=False,
    )
```

```python
import functools

import jax
import jax.numpy as jnp
from jax import lax
from jax.experimental import pallas as pl
from jax.experimental.pallas import tpu as pltpu
from jax.sharding import PartitionSpec as P


BF16 = jnp.bfloat16
F32 = jnp.float32

LIMIT = pltpu.CompilerParams(vmem_limit_bytes=20 << 20)


def shift(block, axis, step):
    devices = range(lax.axis_size(axis))
    return lax.ppermute(block, axis, [(i, i + step) for i in devices if i + step in devices])


def flip(block, axis, bit):
    return lax.ppermute(block, axis, [(i, i ^ bit) for i in range(lax.axis_size(axis))])


def row_pieces(block, dim=1):
    count = lax.axis_size("row")
    if count == 1:
        return [block]
    if count == 2:
        there = flip(block, "row", 1)
        return [block, there]
    return [lax.all_gather(block, "row", axis=dim, tiled=True)]


VMEM = pl.BlockSpec(memory_space=pltpu.VMEM)
HBM = pl.BlockSpec(memory_space=pltpu.HBM)


def mask_body(mask_ref, coupling_ref, out_ref, sems, *, tick):
    block_rows, blocks = mask_ref.shape[2:]
    rows, width = out_ref.shape[1:]
    high, wide = rows // block_rows, width // blocks

    def fetch(k):
        at = pl.ds(k * high, high)
        return pltpu.make_async_copy(coupling_ref.at[tick, 0, :, at, :], out_ref.at[:, at, :], sems.at[k])

    for k in range(block_rows):
        fetch(k).start()
    for k in range(block_rows):
        fetch(k).wait()
        rows_at = slice(k * high, (k + 1) * high)
        for col in range(blocks):
            cols = slice(col * wide, (col + 1) * wide)
            block = out_ref[:, rows_at, cols]
            keep = mask_ref[tick, 0, k, col] != 0
            out_ref[:, rows_at, cols] = jnp.where(keep, block, jnp.zeros_like(block))


def masked_factor(block_mask, coupling, tick):
    rows, width = coupling.shape[3:]
    return pl.pallas_call(
        functools.partial(mask_body, tick=tick),
        grid_spec=pltpu.PrefetchScalarGridSpec(
            num_scalar_prefetch=1,
            grid=(1,),
            in_specs=[HBM],
            out_specs=VMEM,
            scratch_shapes=[pltpu.SemaphoreType.DMA((block_mask.shape[2],))],
        ),
        out_shape=jax.ShapeDtypeStruct((2, rows, width), BF16),
        compiler_params=LIMIT,
    )(block_mask, coupling)


def dot(a, b):
    return jnp.dot(a, b, preferred_element_type=F32)


def dot_t(a, b):
    return lax.dot_general(a, b, (((1,), (1,)), ((), ())), preferred_element_type=F32)


def plan_body(mine, *refs, tick):
    out = refs[-1]
    masks = refs[:-1]
    blocks = masks[0].shape[3]
    one, none = jnp.int32(1), jnp.int32(0)
    rows = []
    for j in range(blocks):
        bits = none
        for c in range(blocks):
            if len(masks) == 1:
                value = masks[0][tick, 0, j, c]
            else:
                half = blocks // 2
                a = masks[0][tick, 0, j % half, c]
                b = masks[1][tick, 0, j % half, c]
                value = jnp.where(mine[0] == j // half, a, b)
            bits = bits + jnp.where(value != 0, jnp.int32(1 << c), none)
        rows.append(bits)

    def widest(start):
        best, found = jnp.int32(-1), none
        for c in range(2, blocks):
            both = start | (1 << c)
            count = none
            for bits in rows:
                count = count + jnp.where((bits & both) == 0, one, none)
            count = jnp.where((start & (1 << c)) != 0, jnp.int32(-1), count)
            found = jnp.where(count > best, jnp.int32(1 << c), found)
            best = jnp.maximum(best, count)
        return found

    last = widest(none)
    near = widest(last)
    soon = none
    for c in range(blocks):
        is_last = (last & (1 << c)) != 0
        is_near = (near & (1 << c)) != 0
        at = jnp.where(is_last, jnp.int32(blocks - 1), jnp.where(is_near, jnp.int32(blocks - 2), soon))
        out[at] = jnp.int32(c)
        soon = soon + jnp.where(jnp.logical_or(is_last, is_near), none, one)
    lead, next_two, rest = none, one, jnp.int32(3)
    for j in range(blocks):
        leads = jnp.logical_and((rows[j] & (last | near)) == 0, lead == 0)
        follows = jnp.logical_and((rows[j] & last) == 0, next_two < 3)
        follows = jnp.logical_and(follows, jnp.logical_not(leads))
        at = jnp.where(leads, none, jnp.where(follows, next_two, jnp.minimum(rest, blocks - 1)))
        out[blocks + at] = jnp.int32(j)
        lead = lead + jnp.where(leads, one, none)
        next_two = next_two + jnp.where(follows, one, none)
        rest = rest + jnp.where(jnp.logical_or(leads, follows), none, one)


def make_plan(mine, masks, tick):
    blocks = masks[0].shape[3]
    smem = pl.BlockSpec(memory_space=pltpu.SMEM)
    return pl.pallas_call(
        functools.partial(plan_body, tick=tick),
        grid_spec=pltpu.PrefetchScalarGridSpec(
            num_scalar_prefetch=1, grid=(1,), in_specs=[smem] * len(masks), out_specs=smem
        ),
        out_shape=jax.ShapeDtypeStruct((2 * blocks,), jnp.int32),
        compiler_params=LIMIT,
        name="plan",
    )(mine, *masks)


SPLIT = 4


def cut_body(mine, here, plan, src, *refs, first, blocks):
    outs, sems = refs[:-1], refs[-1]
    wide = src.shape[3] // blocks if first else outs[0].shape[2]
    copies = []
    for out in outs:
        for u in range(out.shape[2] // wide):
            unit = len(copies) // SPLIT
            at = pl.ds(pl.multiple_of(plan[first + unit] * wide, wide) if first else 0, wide)
            to = slice(u * wide, (u + 1) * wide)
            high = out.shape[1] // SPLIT
            for k in range(SPLIT):
                rows = pl.ds(k * high, high)
                sem = sems.at[SPLIT * unit + k]
                copies.append(pltpu.make_async_copy(src.at[0, :, rows, at], out.at[:, rows, to], sem))
    for copy in copies:
        copy.start()
    for copy in copies:
        copy.wait()


def cut_pieces(mine, here, plan, state, first, sizes, blocks):
    rows, width = state.shape[2:]
    return pl.pallas_call(
        functools.partial(cut_body, first=first, blocks=blocks),
        grid_spec=pltpu.PrefetchScalarGridSpec(
            num_scalar_prefetch=3,
            grid=(1,),
            in_specs=[HBM],
            out_specs=[VMEM] * len(sizes),
            scratch_shapes=[pltpu.SemaphoreType.DMA((SPLIT * sum(sizes),))],
        ),
        out_shape=[jax.ShapeDtypeStruct((2, rows, units * width // blocks), BF16) for units in sizes],
        compiler_params=LIMIT,
    )(mine, here, plan, state)


def fold_body(*refs, pieces, tick, first, kind, base, index, top, count, blocks):
    mine, pidx, pw, here, plan = refs[:5]
    own = refs[5]
    refs = refs[6:]
    factor = refs[:pieces]
    behind = refs[pieces : 2 * pieces]
    before = refs[2 * pieces]
    outs = refs[1 + 2 * pieces :]
    span = behind[0].shape[2]
    wide = own.shape[2] // blocks

    def block_cols(at_block):
        return pl.ds(pl.multiple_of(plan[at_block] * wide, wide), wide)

    def offset(k):
        size = behind[k].shape[1]
        return 0 if pieces == 1 else pl.multiple_of((mine[0] if k == 0 else 1 - mine[0]) * size, size)

    if first:
        green, sem = outs[-2:]
        outs = outs[:-2]
        fetch = pltpu.make_async_copy(before.at[tick, 0], green, sem)
        fetch.start()
    if kind == "final":
        term = outs[-1]
        outs = outs[:-1]
    units = [block_cols(base + u) for u in range(span // wide)]
    tile = min(count, 256)
    for step in range(count // tile):
        at = slice(top + step * tile, top + (step + 1) * tile)
        to = slice(step * tile, (step + 1) * tile)
        both = None
        for k in range(pieces):
            inner = pl.ds(offset(k), behind[k].shape[1])
            left = jnp.concatenate([own[0, at, inner], own[1, at, inner]], axis=0)
            share = dot(left, jnp.concatenate([behind[k][0], behind[k][1]], axis=1))
            both = share if both is None else both + share
        real = both[:tile, :span] - both[tile:, span:]
        imag = both[:tile, span:] + both[tile:, :span]
        left = jnp.concatenate(
            [jnp.concatenate([real, -imag], axis=1), jnp.concatenate([imag, real], axis=1)], axis=0
        ).astype(BF16)
        if first and step == 0:
            fetch.wait()
        for k in range(pieces):
            size = behind[k].shape[1]
            group = min(size, 256)
            for start in range(0, size, group):
                rows = slice(start, start + group)
                right = jnp.concatenate([factor[k][part, rows, cols] for part in range(2) for cols in units], axis=1)
                pair = dot_t(left, right)
                cols = pl.ds(offset(k) + start, group)
                if pieces == 2:
                    cols = pl.ds(pl.multiple_of(offset(k) + start, group), group)
                values = []
                for part in range(2):
                    value = pair[part * tile : (part + 1) * tile]
                    if first:
                        value = green[part, at, cols].astype(F32) + value
                    else:
                        value = before[part, at, cols] + value
                    value = value.astype(outs[0].dtype)
                    outs[0][part, to, cols] = value
                    values.append(value)
                if kind == "final":
                    weighted = weigh_pair(values, pidx, pw, tick)
                    term[0, to, cols] = weighted[0]
                    term[1, to, cols] = weighted[1]
        if kind == "final":
            deal_term(term, here, outs[1:], to)
            continue
        at_block = blocks + index
        for out in outs[1:]:
            for u in range(out.shape[2] // wide):
                for part in range(2):
                    out[part, to, u * wide : (u + 1) * wide] = outs[0][part, to, block_cols(at_block)].astype(BF16)
                at_block += 1


def weigh_pair(values, pidx, pw, tick):
    real, imag = (value.astype(F32) for value in values)
    w0 = pw[0, pidx[0, 0, tick]]
    w1 = pw[1, pidx[0, 0, tick]]
    return (w0 * real - w1 * imag).astype(BF16), (w0 * imag + w1 * real).astype(BF16)


def deal_term(term, here, outs, at):
    if len(outs) == 1:
        outs[0][:, at] = term[:, at]
        return
    real_send, real_keep, imag_send, imag_keep = outs
    quarter = term.shape[2] // 4
    major, minor = here[0] // 2, here[0] % 2

    def cut(part, start, size):
        return term[part, at, pl.ds(pl.multiple_of(start * quarter, quarter), size * quarter)]

    real_send[at] = cut(0, 2 * (1 - major), 2)
    real_keep[at] = cut(0, 2 * major, 2)
    for pair in range(2):
        cols = slice(pair * quarter, (pair + 1) * quarter)
        imag_send[at, cols] = cut(1, 2 * pair + 1 - minor, 1)
        imag_keep[at, cols] = cut(1, 2 * pair + minor, 1)


def term_shapes(rows, width):
    if lax.axis_size("pole") != 4:
        return [jax.ShapeDtypeStruct((2, rows, width), BF16)]
    return [jax.ShapeDtypeStruct((rows, width // 2), BF16)] * 4


def row_parts(rows):
    if rows % 512 or lax.axis_size("pole") != 4:
        return [(0, rows)]
    unit = rows // 4
    return [(0, unit), (unit, 2 * unit), (3 * unit, unit)]


def fold(scalars, own, factor, behind, before, tick, first, kind, base, sends=(), index=0, part=None):
    rows, width = own.shape[1:]
    blocks = scalars[4].shape[0] // 2
    wide = width // blocks
    pieces = len(behind)
    top, count = part or (0, rows)
    done = kind in ("final", "send")
    out_shape = [jax.ShapeDtypeStruct((2, count, width), BF16 if done else F32)]
    out_shape += [jax.ShapeDtypeStruct((2, rows, units * wide), BF16) for units in sends]
    scratch = [pltpu.VMEM((2, rows, width), BF16), pltpu.SemaphoreType.DMA] if first else []
    if kind == "final":
        out_shape += term_shapes(count, width)
        scratch = [pltpu.VMEM((2, count, width), BF16)]
    body = functools.partial(
        fold_body, pieces=pieces, tick=tick, first=first, kind=kind, base=base, index=index, top=top, count=count, blocks=blocks
    )
    return pl.pallas_call(
        body,
        grid_spec=pltpu.PrefetchScalarGridSpec(
            num_scalar_prefetch=len(scalars),
            grid=(1,),
            in_specs=[VMEM] * (1 + 2 * pieces) + [HBM if first else VMEM],
            out_specs=[VMEM] * len(out_shape),
            scratch_shapes=scratch,
        ),
        out_shape=out_shape,
        input_output_aliases={} if first or done else {len(scalars) + 1 + 2 * pieces: 0},
        compiler_params=LIMIT,
    )(*scalars, own, *factor, *behind, before)


def term_body(pidx, pw, here, state, *refs, tick):
    outs, term = refs[:-1], refs[-1]
    rows, width = state.shape[1:]
    tile = min(rows, 128)
    group = min(width, 256)
    for row in range(0, rows, tile):
        at = slice(row, row + tile)
        for col in range(0, width, group):
            cols = slice(col, col + group)
            weighted = weigh_pair([state[part, at, cols] for part in range(2)], pidx, pw, tick)
            term[0, at, cols] = weighted[0]
            term[1, at, cols] = weighted[1]
        deal_term(term, here, outs, at)


def weigh(scalars, state, tick):
    out_shape = term_shapes(*state.shape[1:])
    return pl.pallas_call(
        functools.partial(term_body, tick=tick),
        grid_spec=pltpu.PrefetchScalarGridSpec(
            num_scalar_prefetch=3,
            grid=(1,),
            in_specs=[VMEM],
            out_specs=[VMEM] * len(out_shape),
            scratch_shapes=[pltpu.VMEM(state.shape, BF16)],
        ),
        out_shape=out_shape,
        compiler_params=LIMIT,
    )(*scalars[1:], state)


def emit_body(*refs):
    out, sems = refs[-2:]
    copies = []
    row = 0
    for k, ref in enumerate(refs[:-2]):
        high = ref.shape[1]
        copies.append(pltpu.make_async_copy(ref, out.at[0, :, pl.ds(row, high), :], sems.at[k]))
        row += high
    for copy in copies:
        copy.start()
    for copy in copies:
        copy.wait()


def emit(parts):
    rows, width = sum(part.shape[1] for part in parts), parts[0].shape[2]
    return pl.pallas_call(
        emit_body,
        in_specs=[VMEM] * len(parts),
        out_specs=HBM,
        out_shape=jax.ShapeDtypeStruct((1, 2, rows, width), BF16),
        scratch_shapes=[pltpu.SemaphoreType.DMA((len(parts),))],
        compiler_params=LIMIT,
        name="emit",
    )(*parts)


def picked(ref, which):
    quarter = ref.shape[1] // 2
    return jnp.where(which == 0, ref[:, :quarter], ref[:, quarter:]).astype(F32)


def pass_on_body(here, real_keep, real_got, imag_keep, imag_got, real_send, imag_send):
    major, minor = here[0] // 2, here[0] % 2
    real_send[...] = (picked(real_keep, 1 - minor) + picked(real_got, 1 - minor)).astype(BF16)
    imag_send[...] = (picked(imag_keep, 1 - major) + picked(imag_got, 1 - major)).astype(BF16)


def retain_body(here, *refs, parts, extra):
    major, minor = here[0] // 2, here[0] % 2
    out = refs[-1]
    row = 0
    for k in range(parts):
        real_keep, real_got, imag_keep, imag_got = refs[4 * k : 4 * k + 4]
        at = slice(row, row + real_keep.shape[0])
        row = at.stop
        real = picked(real_keep, minor) + picked(real_got, minor)
        imag = picked(imag_keep, major) + picked(imag_got, major)
        if extra:
            real = refs[4 * parts][0, at] + real
            imag = refs[4 * parts][1, at] + imag
        out[0, at] = real
        out[1, at] = imag


def close_body(base, *refs, top, write):
    if write:
        out, total, sem = refs[-3:]
        lasts = refs[:-4] if top else refs[:-3]
        row = top
    else:
        total = refs[-1]
        lasts = refs[:-1]
        row = 0
    first = row
    for k in range(len(lasts) // 2):
        at = slice(row, row + lasts[2 * k].shape[0])
        to = slice(row - first, at.stop - first)
        row = at.stop
        total[0, to] = base[0, at] + lasts[2 * k][...].astype(F32)
        total[1, to] = base[1, at] + lasts[2 * k + 1][...].astype(F32)
    if write:
        copy = pltpu.make_async_copy(total, out.at[:, pl.ds(first, row - first), :], sem)
        copy.start()
        copy.wait()


def close_out(base, lasts, top, whole):
    high = sum(last.shape[0] for last in lasts[::2])
    args = [base, *lasts] + ([whole] if top else [])
    return pl.pallas_call(
        functools.partial(close_body, top=top, write=True),
        in_specs=[VMEM] * (1 + len(lasts)) + ([HBM] if top else []),
        out_specs=HBM,
        out_shape=jax.ShapeDtypeStruct(base.shape, F32),
        scratch_shapes=[pltpu.VMEM((2, high, base.shape[2]), F32), pltpu.SemaphoreType.DMA],
        input_output_aliases={len(args) - 1: 0} if top else {},
        compiler_params=LIMIT,
    )(*args)


def kernel_call(fn, scalars, args, out_shape):
    many = isinstance(out_shape, list)
    return pl.pallas_call(
        fn,
        grid_spec=pltpu.PrefetchScalarGridSpec(
            num_scalar_prefetch=len(scalars),
            grid=(1,),
            in_specs=[VMEM] * len(args),
            out_specs=[VMEM] * len(out_shape) if many else VMEM,
        ),
        out_shape=out_shape,
        compiler_params=LIMIT,
    )(*scalars, *args)


def scatter_sum(terms, before, here, last):
    if len(terms[0]) == 1:
        share = lax.psum_scatter(terms[0][0], "pole", scatter_dimension=2, tiled=True).astype(F32)
        return share if before is None else before + share
    fields = []
    for real_out, real_keep, imag_out, imag_keep in terms:
        real_got = flip(real_out, "pole", 2)
        imag_got = flip(imag_out, "pole", 1)
        fields.append((real_keep, real_got, imag_keep, imag_got))
    lasts = []
    for field in fields:
        high, half = field[0].shape
        send = jax.ShapeDtypeStruct((high, half // 2), BF16)
        sends = kernel_call(pass_on_body, (here,), field, [send] * 2)
        real_last = flip(sends[0], "pole", 1)
        imag_last = flip(sends[1], "pole", 2)
        lasts.append((real_last, imag_last))
    extra = [] if before is None else [before]
    rows = sum(field[0].shape[0] for field in fields)
    shape = jax.ShapeDtypeStruct((2, rows, half // 2), F32)
    flat = [value for field in fields for value in field]
    retain = functools.partial(retain_body, parts=len(fields), extra=len(extra))
    base = kernel_call(retain, (here,), flat + extra, shape)
    if not last:
        close = functools.partial(close_body, top=0, write=False)
        return kernel_call(close, (), [base, *(v for pair in lasts for v in pair)], shape)
    whole = None
    top = 0
    groups = [lasts[:-1], lasts[-1:]] if len(lasts) > 1 else [lasts]
    for group in groups:
        flat = [value for pair in group for value in pair]
        whole = close_out(base, flat, top, whole)
        top += sum(pair[0].shape[0] for pair in group)
    return whole


ARRIVE = (2, 2, 1, 1, 1, 1)
LEAVE = (1, 2, 2, 2, 1)


def body(local_green, coupling, block_mask, state_in, pole_weight, pole_index):
    local_green, coupling, state_in = (
        pltpu.with_memory_space_constraint(value, pltpu.HBM) for value in (local_green, coupling, state_in)
    )
    ticks = coupling.shape[0]
    blocks = block_mask.shape[3]
    here = jnp.reshape(lax.axis_index("pole").astype(jnp.int32), (1,))
    mine = jnp.reshape(lax.axis_index("row").astype(jnp.int32), (1,))
    masks = row_pieces(block_mask, 2)
    state = cut_pieces(mine, here, mine, state_in, 0, ARRIVE[:1], blocks)
    plan = make_plan(mine, masks, 0)
    plan_up = shift(plan, "slab", 1)
    plan_down = shift(plan, "slab", -1)
    state += cut_pieces(mine, here, plan_up, state_in, ARRIVE[0], ARRIVE[1:2], blocks)
    state += cut_pieces(mine, here, plan_up, state_in, sum(ARRIVE[:2]), ARRIVE[2:], blocks)
    owns = []
    factors = []
    for tick in range(ticks):
        own = masked_factor(block_mask, coupling, tick)
        owns.append(own)
        factors.append(row_pieces(own))
    weights = (mine, jnp.transpose(pole_index, (1, 2, 0)), pole_weight, here)
    density = None
    incoming = []
    for piece in state:
        incoming.append(shift(piece, "slab", -1))
    for tick in range(ticks):
        own, factor = owns[tick], factors[tick]
        scalars = (*weights, plan_down if tick else plan)
        base = blocks if tick else 0
        before = local_green
        last_tick = tick == ticks - 1
        leaving = []
        for c, piece in enumerate(incoming):
            behind = row_pieces(piece)
            last = c == len(incoming) - 1
            kind, sends, index = "sum", (), 0
            if not last_tick and len(incoming) - c <= 3:
                kind = "send" if last else "sum"
                index = sum(LEAVE[: len(leaving)])
                sends = LEAVE[len(leaving) :] if last else LEAVE[len(leaving) : len(leaving) + 1]
            if last_tick and last:
                break
            outs = fold(scalars, own, factor, behind, before, tick, c == 0, kind, base, sends, index)
            before = outs[0]
            base += piece.shape[2] * blocks // own.shape[2]
            for block in outs[1:]:
                leaving.append(shift(block, "slab", -1))
        if last_tick:
            finals = []
            terms = []
            for part in row_parts(own.shape[1]):
                outs = fold(scalars, own, factor, behind, before, tick, False, "final", base, part=part)
                finals.append(outs[0])
                terms.append(outs[1:])
            density = scatter_sum(terms, density, here, True)
            state_out = emit(finals)
        else:
            terms = weigh(scalars[:4], before, tick)
            density = scatter_sum([terms], density, here, False)
        incoming = leaving
    return (state_out, density)


def solution(mesh):
    placed = (
        P(None, "pole", None, ("slab", "row"), None),
        P(None, "pole", None, ("slab", "row"), None),
        P(None, "pole", ("slab", "row"), None),
        P("pole", None, ("slab", "row"), None),
        P(),
        P(None, "pole", "slab"),
    )
    return jax.shard_map(
        body,
        mesh=mesh,
        in_specs=placed,
        out_specs=(P("pole", None, ("slab", "row"), None), P(None, ("slab", "row"), "pole")),
        check_vma=False,
    )
```

```python
import functools

import jax
import jax.numpy as jnp
from jax import lax
from jax.experimental import pallas as pl
from jax.experimental.pallas import tpu as pltpu
from jax.sharding import PartitionSpec as P


BF16 = jnp.bfloat16
F32 = jnp.float32

LIMIT = pltpu.CompilerParams(vmem_limit_bytes=20 << 20)


def shift(block, axis, step):
    devices = range(lax.axis_size(axis))
    return lax.ppermute(block, axis, [(i, i + step) for i in devices if i + step in devices])


def flip(block, axis, bit):
    return lax.ppermute(block, axis, [(i, i ^ bit) for i in range(lax.axis_size(axis))])


def row_pieces(block, dim=1):
    count = lax.axis_size("row")
    if count == 1:
        return [block]
    if count == 2:
        there = flip(block, "row", 1)
        return [block, there]
    return [lax.all_gather(block, "row", axis=dim, tiled=True)]


VMEM = pl.BlockSpec(memory_space=pltpu.VMEM)
HBM = pl.BlockSpec(memory_space=pltpu.HBM)


def mask_body(mask_ref, coupling_ref, out_ref, sems, *, tick):
    block_rows, blocks = mask_ref.shape[2:]
    rows, width = out_ref.shape[1:]
    high, wide = rows // block_rows, width // blocks

    def fetch(k):
        at = pl.ds(k * high, high)
        return pltpu.make_async_copy(coupling_ref.at[tick, 0, :, at, :], out_ref.at[:, at, :], sems.at[k])

    for k in range(block_rows):
        fetch(k).start()
    for k in range(block_rows):
        fetch(k).wait()
        rows_at = slice(k * high, (k + 1) * high)
        for col in range(blocks):
            cols = slice(col * wide, (col + 1) * wide)
            block = out_ref[:, rows_at, cols]
            keep = mask_ref[tick, 0, k, col] != 0
            out_ref[:, rows_at, cols] = jnp.where(keep, block, jnp.zeros_like(block))


def masked_factor(block_mask, coupling, tick):
    rows, width = coupling.shape[3:]
    return pl.pallas_call(
        functools.partial(mask_body, tick=tick),
        grid_spec=pltpu.PrefetchScalarGridSpec(
            num_scalar_prefetch=1,
            grid=(1,),
            in_specs=[HBM],
            out_specs=VMEM,
            scratch_shapes=[pltpu.SemaphoreType.DMA((block_mask.shape[2],))],
        ),
        out_shape=jax.ShapeDtypeStruct((2, rows, width), BF16),
        compiler_params=LIMIT,
    )(block_mask, coupling)


def dot(a, b):
    return jnp.dot(a, b, preferred_element_type=F32)


def dot_t(a, b):
    return lax.dot_general(a, b, (((1,), (1,)), ((), ())), preferred_element_type=F32)


def plan_body(mine, *refs, tick):
    out = refs[-1]
    masks = refs[:-1]
    blocks = masks[0].shape[3]
    one, none = jnp.int32(1), jnp.int32(0)
    rows = []
    for j in range(blocks):
        bits = none
        for c in range(blocks):
            if len(masks) == 1:
                value = masks[0][tick, 0, j, c]
            else:
                half = blocks // 2
                a = masks[0][tick, 0, j % half, c]
                b = masks[1][tick, 0, j % half, c]
                value = jnp.where(mine[0] == j // half, a, b)
            bits = bits + jnp.where(value != 0, jnp.int32(1 << c), none)
        rows.append(bits)

    def widest(start):
        best, found = jnp.int32(-1), none
        for c in range(2, blocks):
            both = start | (1 << c)
            count = none
            for bits in rows:
                count = count + jnp.where((bits & both) == 0, one, none)
            count = jnp.where((start & (1 << c)) != 0, jnp.int32(-1), count)
            found = jnp.where(count > best, jnp.int32(1 << c), found)
            best = jnp.maximum(best, count)
        return found

    last = widest(none)
    near = widest(last)
    soon = none
    for c in range(blocks):
        is_last = (last & (1 << c)) != 0
        is_near = (near & (1 << c)) != 0
        at = jnp.where(is_last, jnp.int32(blocks - 1), jnp.where(is_near, jnp.int32(blocks - 2), soon))
        out[at] = jnp.int32(c)
        soon = soon + jnp.where(jnp.logical_or(is_last, is_near), none, one)
    lead, next_two, rest = none, one, jnp.int32(3)
    for j in range(blocks):
        leads = jnp.logical_and((rows[j] & (last | near)) == 0, lead == 0)
        follows = jnp.logical_and((rows[j] & last) == 0, next_two < 3)
        follows = jnp.logical_and(follows, jnp.logical_not(leads))
        at = jnp.where(leads, none, jnp.where(follows, next_two, jnp.minimum(rest, blocks - 1)))
        out[blocks + at] = jnp.int32(j)
        lead = lead + jnp.where(leads, one, none)
        next_two = next_two + jnp.where(follows, one, none)
        rest = rest + jnp.where(jnp.logical_or(leads, follows), none, one)


def make_plan(mine, masks, tick):
    blocks = masks[0].shape[3]
    smem = pl.BlockSpec(memory_space=pltpu.SMEM)
    return pl.pallas_call(
        functools.partial(plan_body, tick=tick),
        grid_spec=pltpu.PrefetchScalarGridSpec(
            num_scalar_prefetch=1, grid=(1,), in_specs=[smem] * len(masks), out_specs=smem
        ),
        out_shape=jax.ShapeDtypeStruct((2 * blocks,), jnp.int32),
        compiler_params=LIMIT,
        name="plan",
    )(mine, *masks)


SPLIT = 1


def cut_body(mine, here, plan, src, *refs, first, blocks):
    outs, sems = refs[:-1], refs[-1]
    wide = src.shape[3] // blocks if first else outs[0].shape[2]
    copies = []
    for out in outs:
        for u in range(out.shape[2] // wide):
            unit = len(copies) // SPLIT
            at = pl.ds(pl.multiple_of(plan[first + unit] * wide, wide) if first else 0, wide)
            to = slice(u * wide, (u + 1) * wide)
            high = out.shape[1] // SPLIT
            for k in range(SPLIT):
                rows = pl.ds(k * high, high)
                sem = sems.at[SPLIT * unit + k]
                copies.append(pltpu.make_async_copy(src.at[0, :, rows, at], out.at[:, rows, to], sem))
    for copy in copies:
        copy.start()
    for copy in copies:
        copy.wait()


def cut_pieces(mine, here, plan, state, first, sizes, blocks):
    rows, width = state.shape[2:]
    return pl.pallas_call(
        functools.partial(cut_body, first=first, blocks=blocks),
        grid_spec=pltpu.PrefetchScalarGridSpec(
            num_scalar_prefetch=3,
            grid=(1,),
            in_specs=[HBM],
            out_specs=[VMEM] * len(sizes),
            scratch_shapes=[pltpu.SemaphoreType.DMA((SPLIT * sum(sizes),))],
        ),
        out_shape=[jax.ShapeDtypeStruct((2, rows, units * width // blocks), BF16) for units in sizes],
        compiler_params=LIMIT,
    )(mine, here, plan, state)


def fold_body(*refs, pieces, tick, first, kind, base, index, top, count, blocks):
    mine, pidx, pw, here, plan = refs[:5]
    own = refs[5]
    refs = refs[6:]
    factor = refs[:pieces]
    behind = refs[pieces : 2 * pieces]
    before = refs[2 * pieces]
    outs = refs[1 + 2 * pieces :]
    span = behind[0].shape[2]
    wide = own.shape[2] // blocks

    def block_cols(at_block):
        return pl.ds(pl.multiple_of(plan[at_block] * wide, wide), wide)

    def offset(k):
        size = behind[k].shape[1]
        return 0 if pieces == 1 else pl.multiple_of((mine[0] if k == 0 else 1 - mine[0]) * size, size)

    if first:
        green, sem = outs[-2:]
        outs = outs[:-2]
        fetch = pltpu.make_async_copy(before.at[tick, 0], green, sem)
        fetch.start()
    if kind == "final":
        term = outs[-1]
        outs = outs[:-1]
    units = [block_cols(base + u) for u in range(span // wide)]
    tile = min(count, 512)
    for step in range(count // tile):
        at = slice(top + step * tile, top + (step + 1) * tile)
        to = slice(step * tile, (step + 1) * tile)
        both = None
        for k in range(pieces):
            inner = pl.ds(offset(k), behind[k].shape[1])
            left = jnp.concatenate([own[0, at, inner], own[1, at, inner]], axis=0)
            share = dot(left, jnp.concatenate([behind[k][0], behind[k][1]], axis=1))
            both = share if both is None else both + share
        real = both[:tile, :span] - both[tile:, span:]
        imag = both[:tile, span:] + both[tile:, :span]
        left = jnp.concatenate(
            [jnp.concatenate([real, -imag], axis=1), jnp.concatenate([imag, real], axis=1)], axis=0
        ).astype(BF16)
        if first and step == 0:
            fetch.wait()
        for k in range(pieces):
            size = behind[k].shape[1]
            group = min(size, 256)
            for start in range(0, size, group):
                rows = slice(start, start + group)
                right = jnp.concatenate([factor[k][part, rows, cols] for part in range(2) for cols in units], axis=1)
                pair = dot_t(left, right)
                cols = pl.ds(offset(k) + start, group)
                if pieces == 2:
                    cols = pl.ds(pl.multiple_of(offset(k) + start, group), group)
                values = []
                for part in range(2):
                    value = pair[part * tile : (part + 1) * tile]
                    if first:
                        value = green[part, at, cols].astype(F32) + value
                    else:
                        value = before[part, at, cols] + value
                    value = value.astype(outs[0].dtype)
                    outs[0][part, to, cols] = value
                    values.append(value)
                if kind == "final":
                    weighted = weigh_pair(values, pidx, pw, tick)
                    term[0, to, cols] = weighted[0]
                    term[1, to, cols] = weighted[1]
        if kind == "final":
            deal_term(term, here, outs[1:], to)
            continue
        at_block = blocks + index
        for out in outs[1:]:
            for u in range(out.shape[2] // wide):
                for part in range(2):
                    out[part, to, u * wide : (u + 1) * wide] = outs[0][part, to, block_cols(at_block)].astype(BF16)
                at_block += 1


def weigh_pair(values, pidx, pw, tick):
    real, imag = (value.astype(F32) for value in values)
    w0 = pw[0, pidx[0, 0, tick]]
    w1 = pw[1, pidx[0, 0, tick]]
    return (w0 * real - w1 * imag).astype(BF16), (w0 * imag + w1 * real).astype(BF16)


def deal_term(term, here, outs, at):
    if len(outs) == 1:
        outs[0][:, at] = term[:, at]
        return
    real_send, real_keep, imag_send, imag_keep = outs
    quarter = term.shape[2] // 4
    major, minor = here[0] // 2, here[0] % 2

    def cut(part, start, size):
        return term[part, at, pl.ds(pl.multiple_of(start * quarter, quarter), size * quarter)]

    real_send[at] = cut(0, 2 * (1 - major), 2)
    real_keep[at] = cut(0, 2 * major, 2)
    for pair in range(2):
        cols = slice(pair * quarter, (pair + 1) * quarter)
        imag_send[at, cols] = cut(1, 2 * pair + 1 - minor, 1)
        imag_keep[at, cols] = cut(1, 2 * pair + minor, 1)


def term_shapes(rows, width):
    if lax.axis_size("pole") != 4:
        return [jax.ShapeDtypeStruct((2, rows, width), BF16)]
    return [jax.ShapeDtypeStruct((rows, width // 2), BF16)] * 4


def row_parts(rows):
    if rows % 512 or lax.axis_size("pole") != 4:
        return [(0, rows)]
    return [(0, rows // 2), (rows // 2, rows // 2)]


def fold(scalars, own, factor, behind, before, tick, first, kind, base, sends=(), index=0, part=None):
    rows, width = own.shape[1:]
    blocks = scalars[4].shape[0] // 2
    wide = width // blocks
    pieces = len(behind)
    top, count = part or (0, rows)
    done = kind in ("final", "send")
    out_shape = [jax.ShapeDtypeStruct((2, count, width), BF16 if done else F32)]
    out_shape += [jax.ShapeDtypeStruct((2, rows, units * wide), BF16) for units in sends]
    scratch = [pltpu.VMEM((2, rows, width), BF16), pltpu.SemaphoreType.DMA] if first else []
    if kind == "final":
        out_shape += term_shapes(count, width)
        scratch = [pltpu.VMEM((2, count, width), BF16)]
    body = functools.partial(
        fold_body, pieces=pieces, tick=tick, first=first, kind=kind, base=base, index=index, top=top, count=count, blocks=blocks
    )
    return pl.pallas_call(
        body,
        grid_spec=pltpu.PrefetchScalarGridSpec(
            num_scalar_prefetch=len(scalars),
            grid=(1,),
            in_specs=[VMEM] * (1 + 2 * pieces) + [HBM if first else VMEM],
            out_specs=[VMEM] * len(out_shape),
            scratch_shapes=scratch,
        ),
        out_shape=out_shape,
        input_output_aliases={} if first or done else {len(scalars) + 1 + 2 * pieces: 0},
        compiler_params=LIMIT,
    )(*scalars, own, *factor, *behind, before)


def term_body(pidx, pw, here, state, *refs, tick):
    outs, term = refs[:-1], refs[-1]
    rows, width = state.shape[1:]
    tile = min(rows, 128)
    group = min(width, 256)
    for row in range(0, rows, tile):
        at = slice(row, row + tile)
        for col in range(0, width, group):
            cols = slice(col, col + group)
            weighted = weigh_pair([state[part, at, cols] for part in range(2)], pidx, pw, tick)
            term[0, at, cols] = weighted[0]
            term[1, at, cols] = weighted[1]
        deal_term(term, here, outs, at)


def weigh(scalars, state, tick):
    out_shape = term_shapes(*state.shape[1:])
    return pl.pallas_call(
        functools.partial(term_body, tick=tick),
        grid_spec=pltpu.PrefetchScalarGridSpec(
            num_scalar_prefetch=3,
            grid=(1,),
            in_specs=[VMEM],
            out_specs=[VMEM] * len(out_shape),
            scratch_shapes=[pltpu.VMEM(state.shape, BF16)],
        ),
        out_shape=out_shape,
        compiler_params=LIMIT,
    )(*scalars[1:], state)


def emit_body(*refs):
    out, sems = refs[-2:]
    copies = []
    row = 0
    for k, ref in enumerate(refs[:-2]):
        high = ref.shape[1]
        copies.append(pltpu.make_async_copy(ref, out.at[0, :, pl.ds(row, high), :], sems.at[k]))
        row += high
    for copy in copies:
        copy.start()
    for copy in copies:
        copy.wait()


def emit(parts):
    rows, width = sum(part.shape[1] for part in parts), parts[0].shape[2]
    return pl.pallas_call(
        emit_body,
        in_specs=[VMEM] * len(parts),
        out_specs=HBM,
        out_shape=jax.ShapeDtypeStruct((1, 2, rows, width), BF16),
        scratch_shapes=[pltpu.SemaphoreType.DMA((len(parts),))],
        compiler_params=LIMIT,
        name="emit",
    )(*parts)


def picked(ref, which):
    quarter = ref.shape[1] // 2
    return jnp.where(which == 0, ref[:, :quarter], ref[:, quarter:]).astype(F32)


def pass_on_body(here, real_keep, real_got, imag_keep, imag_got, real_send, imag_send):
    major, minor = here[0] // 2, here[0] % 2
    real_send[...] = (picked(real_keep, 1 - minor) + picked(real_got, 1 - minor)).astype(BF16)
    imag_send[...] = (picked(imag_keep, 1 - major) + picked(imag_got, 1 - major)).astype(BF16)


def retain_body(here, *refs, parts, extra):
    major, minor = here[0] // 2, here[0] % 2
    out = refs[-1]
    row = 0
    for k in range(parts):
        real_keep, real_got, imag_keep, imag_got = refs[4 * k : 4 * k + 4]
        at = slice(row, row + real_keep.shape[0])
        row = at.stop
        real = picked(real_keep, minor) + picked(real_got, minor)
        imag = picked(imag_keep, major) + picked(imag_got, major)
        if extra:
            real = refs[4 * parts][0, at] + real
            imag = refs[4 * parts][1, at] + imag
        out[0, at] = real
        out[1, at] = imag


def close_body(base, *refs, top, write):
    if write:
        out, total, sem = refs[-3:]
        lasts = refs[:-4] if top else refs[:-3]
        row = top
    else:
        total = refs[-1]
        lasts = refs[:-1]
        row = 0
    first = row
    for k in range(len(lasts) // 2):
        at = slice(row, row + lasts[2 * k].shape[0])
        to = slice(row - first, at.stop - first)
        row = at.stop
        total[0, to] = base[0, at] + lasts[2 * k][...].astype(F32)
        total[1, to] = base[1, at] + lasts[2 * k + 1][...].astype(F32)
    if write:
        copy = pltpu.make_async_copy(total, out.at[:, pl.ds(first, row - first), :], sem)
        copy.start()
        copy.wait()


def close_out(base, lasts, top, whole):
    high = sum(last.shape[0] for last in lasts[::2])
    args = [base, *lasts] + ([whole] if top else [])
    return pl.pallas_call(
        functools.partial(close_body, top=top, write=True),
        in_specs=[VMEM] * (1 + len(lasts)) + ([HBM] if top else []),
        out_specs=HBM,
        out_shape=jax.ShapeDtypeStruct(base.shape, F32),
        scratch_shapes=[pltpu.VMEM((2, high, base.shape[2]), F32), pltpu.SemaphoreType.DMA],
        input_output_aliases={len(args) - 1: 0} if top else {},
        compiler_params=LIMIT,
    )(*args)


def kernel_call(fn, scalars, args, out_shape):
    many = isinstance(out_shape, list)
    return pl.pallas_call(
        fn,
        grid_spec=pltpu.PrefetchScalarGridSpec(
            num_scalar_prefetch=len(scalars),
            grid=(1,),
            in_specs=[VMEM] * len(args),
            out_specs=[VMEM] * len(out_shape) if many else VMEM,
        ),
        out_shape=out_shape,
        compiler_params=LIMIT,
    )(*scalars, *args)


def scatter_sum(terms, before, here, last):
    if len(terms[0]) == 1:
        share = lax.psum_scatter(terms[0][0], "pole", scatter_dimension=2, tiled=True).astype(F32)
        return share if before is None else before + share
    fields = []
    for real_out, real_keep, imag_out, imag_keep in terms:
        real_got = flip(real_out, "pole", 2)
        imag_got = flip(imag_out, "pole", 1)
        fields.append((real_keep, real_got, imag_keep, imag_got))
    lasts = []
    for field in fields:
        high, half = field[0].shape
        send = jax.ShapeDtypeStruct((high, half // 2), BF16)
        sends = kernel_call(pass_on_body, (here,), field, [send] * 2)
        real_last = flip(sends[0], "pole", 1)
        imag_last = flip(sends[1], "pole", 2)
        lasts.append((real_last, imag_last))
    extra = [] if before is None else [before]
    rows = sum(field[0].shape[0] for field in fields)
    shape = jax.ShapeDtypeStruct((2, rows, half // 2), F32)
    flat = [value for field in fields for value in field]
    retain = functools.partial(retain_body, parts=len(fields), extra=len(extra))
    base = kernel_call(retain, (here,), flat + extra, shape)
    if not last:
        close = functools.partial(close_body, top=0, write=False)
        return kernel_call(close, (), [base, *(v for pair in lasts for v in pair)], shape)
    whole = None
    top = 0
    groups = [lasts[:-1], lasts[-1:]] if len(lasts) > 1 else [lasts]
    for group in groups:
        flat = [value for pair in group for value in pair]
        whole = close_out(base, flat, top, whole)
        top += sum(pair[0].shape[0] for pair in group)
    return whole


ARRIVE = (2, 2, 1, 1, 1, 1)
LEAVE = (1, 2, 2, 1, 1, 1)


def body(local_green, coupling, block_mask, state_in, pole_weight, pole_index):
    local_green, coupling, state_in = (
        pltpu.with_memory_space_constraint(value, pltpu.HBM) for value in (local_green, coupling, state_in)
    )
    ticks = coupling.shape[0]
    blocks = block_mask.shape[3]
    here = jnp.reshape(lax.axis_index("pole").astype(jnp.int32), (1,))
    mine = jnp.reshape(lax.axis_index("row").astype(jnp.int32), (1,))
    masks = row_pieces(block_mask, 2)
    state = cut_pieces(mine, here, mine, state_in, 0, ARRIVE[:1], blocks)
    plan = make_plan(mine, masks, 0)
    plan_up = shift(plan, "slab", 1)
    plan_down = shift(plan, "slab", -1)
    state += cut_pieces(mine, here, plan_up, state_in, ARRIVE[0], ARRIVE[1:2], blocks)
    state += cut_pieces(mine, here, plan_up, state_in, sum(ARRIVE[:2]), ARRIVE[2:], blocks)
    owns = []
    factors = []
    for tick in range(ticks):
        own = masked_factor(block_mask, coupling, tick)
        owns.append(own)
        factors.append(row_pieces(own))
    weights = (mine, jnp.transpose(pole_index, (1, 2, 0)), pole_weight, here)
    density = None
    incoming = []
    for piece in state:
        incoming.append(shift(piece, "slab", -1))
    for tick in range(ticks):
        own, factor = owns[tick], factors[tick]
        scalars = (*weights, plan_down if tick else plan)
        base = blocks if tick else 0
        before = local_green
        last_tick = tick == ticks - 1
        leaving = []
        for c, piece in enumerate(incoming):
            behind = row_pieces(piece)
            last = c == len(incoming) - 1
            kind, sends, index = "sum", (), 0
            if not last_tick and len(incoming) - c <= 3:
                kind = "send" if last else "sum"
                index = sum(LEAVE[: len(leaving)])
                sends = LEAVE[len(leaving) :] if last else LEAVE[len(leaving) : len(leaving) + 1]
            if last_tick and last:
                break
            outs = fold(scalars, own, factor, behind, before, tick, c == 0, kind, base, sends, index)
            before = outs[0]
            base += piece.shape[2] * blocks // own.shape[2]
            for block in outs[1:]:
                leaving.append(shift(block, "slab", -1))
        if last_tick:
            finals = []
            terms = []
            for part in row_parts(own.shape[1]):
                outs = fold(scalars, own, factor, behind, before, tick, False, "final", base, part=part)
                finals.append(outs[0])
                terms.append(outs[1:])
            density = scatter_sum(terms, density, here, True)
            state_out = emit(finals)
        else:
            terms = weigh(scalars[:4], before, tick)
            density = scatter_sum([terms], density, here, False)
        incoming = leaving
    return (state_out, density)


def solution(mesh):
    placed = (
        P(None, "pole", None, ("slab", "row"), None),
        P(None, "pole", None, ("slab", "row"), None),
        P(None, "pole", ("slab", "row"), None),
        P("pole", None, ("slab", "row"), None),
        P(),
        P(None, "pole", "slab"),
    )
    return jax.shard_map(
        body,
        mesh=mesh,
        in_specs=placed,
        out_specs=(P("pole", None, ("slab", "row"), None), P(None, ("slab", "row"), "pole")),
        check_vma=False,
    )
```
